128 devices in a mesh: seq: 16 (over y, z), head: 8 (over x, core).
Axes of the slice: x: 4, y: 4, z: 4, core: 2. Of those that a mesh axis runs over, the one named last changes fastest.
Arguments:
- inputs: bfloat16 [4096, 6144], P('seq'), may hold values from -6 to 6
- w_query: bfloat16 [6144, 4096], P(None, 'head'), may hold values from -0.078125 to 0.078125
- w_key: bfloat16 [6144, 4096], P(None, 'head'), may hold values from -0.078125 to 0.078125
- w_value: bfloat16 [6144, 4096], P(None, 'head'), may hold values from -0.078125 to 0.078125
- state_in: float32 [32, 128, 128], P('head'), may hold values from -6 to 6
- grad_out: bfloat16 [4096, 4096], P('seq', 'head'), may hold values from -1.5 to 1.5
Outputs:
- attended: bfloat16 [4096, 4096], P('seq', 'head')
- grad_wq: bfloat16 [6144, 4096], P('seq', 'head')
- grad_wk: bfloat16 [6144, 4096], P('seq', 'head')
- grad_wv: bfloat16 [6144, 4096], P('seq', 'head')
- grad_x: bfloat16 [4096, 6144], P('seq', 'head')
The draws below stay inside these ranges and needn't reach their ends.
All inputs are finite; a program needn't handle non-finite values.
Results may differ from the reference program's by a relative error of at most 0.018.
Values may be sent and summed in bfloat16 or wider, within the bound.
No kernel may reach another device: no remote copies, remote signals or barrier semaphores. Data moves between devices by JAX's collectives and lax.ppermute only.
A program may use at most 128 MiB of HBM per device.

```python
import jax
import jax.numpy as jnp
from jax import lax

D = 6144
HEADS = 32
HEAD_DIM = 128
TOK_DEV = 256
TOKENS = 4096
HEADS_DEV = 4
N_SEQ = 16
N_HEAD = 8


def spiked(values, own_key, source, target, parts, factor):
    owner, partner = [(jnp.arange(values.shape[axis_at]) // (values.shape[axis_at] // parts)).reshape([-1 if axis == axis_at else 1 for axis in range(values.ndim)]) for axis_at in (source, target)]
    chosen = jax.random.permutation(own_key, parts)[partner]
    strong = (owner == chosen) | (owner == (partner + parts // 2) % parts)
    return jnp.where(strong, factor * values, values)


def shard_levels(stream_key, extent, split, low, high):
    level = 1.0
    for position, shards_of in split:
        draws = jax.random.uniform(jax.random.fold_in(jax.random.fold_in(stream_key, 6), position), (shards_of,), jnp.float32, low / len(split), high / len(split))
        level = level * jnp.repeat(jnp.exp(draws), extent[position] // shards_of).reshape((-1,) + (1,) * (len(extent) - 1 - position))
    return level


def gaussian(key, shape, spread, reach, split=(), held_as=jnp.bfloat16):
    gain = shard_levels(key, shape, split, -0.22, 0.18) if split else 1.0
    drawn = jax.random.normal(key, shape, jnp.float32) * spread * gain
    return jnp.minimum(jnp.maximum(drawn, -reach), reach).astype(held_as)


def gaussian_with(own_key, dims, scale, reach, pieces, heavy, held_as=jnp.bfloat16):
    array = scale * jax.random.normal(own_key, dims, jnp.float32)
    if pieces:
        array = array * shard_levels(own_key, dims, pieces, -0.22, 0.18)
    return jnp.clip(spiked(array, jax.random.fold_in(own_key, 3), *heavy), -reach, reach).astype(held_as)


def setup_inputs(seed: int = 0) -> dict:
    arg_keys = jax.random.split(jax.random.key(seed), 7)
    return {
        "inputs": gaussian_with(arg_keys[0], (TOKENS, D), 1.0, 6.0, ((0, 16),), (0, 1, 16, 2.0)),
        "w_query": gaussian(arg_keys[1], (D, HEADS * HEAD_DIM), D ** -0.5, 0.078125, ((1, 8),)),
        "w_key": gaussian(arg_keys[2], (D, HEADS * HEAD_DIM), D ** -0.5, 0.078125, ((1, 8),)),
        "w_value": gaussian(arg_keys[3], (D, HEADS * HEAD_DIM), D ** -0.5, 0.078125, ((1, 8),)),
        "state_in": gaussian(arg_keys[4], (HEADS, HEAD_DIM, HEAD_DIM), 1.0, 6.0, ((0, 8),), jnp.float32),
        "grad_out": gaussian(arg_keys[5], (TOKENS, HEADS * HEAD_DIM), 0.25, 1.5, ((0, 16), (1, 8))),
    }


def reference(inputs, w_query, w_key, w_value, state_in, grad_out):
    single_precision = jnp.float32
    bf16 = jnp.bfloat16
    q_scale = HEAD_DIM ** -0.5
    k_scale = TOKENS ** -0.5
    query = (jnp.dot(inputs, w_query, preferred_element_type=single_precision) * q_scale).astype(bf16)
    key = (jnp.dot(inputs, w_key, preferred_element_type=single_precision) * k_scale).astype(bf16)
    value = jnp.dot(inputs, w_value, preferred_element_type=single_precision).astype(bf16)
    shape4 = (N_SEQ, TOK_DEV, HEADS, HEAD_DIM)
    qf = query.reshape(shape4).astype(single_precision)
    kf = key.reshape(shape4).astype(single_precision)
    vf = value.reshape(shape4).astype(single_precision)
    gf = grad_out.reshape(shape4).astype(single_precision)
    block_state = jnp.einsum('clhi,clhj->chij', kf, vf)
    inclusive = jnp.cumsum(block_state, axis=0)
    prior = state_in[None].astype(single_precision) + (inclusive - block_state)
    prior_low = prior.astype(bf16).astype(single_precision)
    mask = jnp.tril(jnp.ones((TOK_DEV, TOK_DEV), dtype=bool))
    causal_mask = jnp.where(mask, jnp.einsum('clhd,cmhd->chlm', qf, kf), 0.0).astype(bf16).astype(single_precision)
    attended = jnp.einsum('chlm,cmhd->clhd', causal_mask, vf) + jnp.einsum('clhi,chij->clhj', qf, prior_low)
    attended = attended.astype(bf16).reshape(TOKENS, HEADS * HEAD_DIM)
    block_adjoint = jnp.einsum('clhi,clhj->chij', qf, gf)
    rev_incl = jnp.cumsum(block_adjoint[::-1], axis=0)[::-1]
    later = rev_incl - block_adjoint
    later_low = later.astype(bf16).astype(single_precision)
    backward_causal_mask = jnp.where(mask, jnp.einsum('clhd,cmhd->chlm', gf, vf), 0.0).astype(bf16).astype(single_precision)
    query_gradient = (jnp.einsum('chlm,cmhd->clhd', backward_causal_mask, kf) + jnp.einsum('clhj,chij->clhi', gf, prior_low)) * q_scale
    key_gradient = (jnp.einsum('chlm,clhd->cmhd', backward_causal_mask, qf) + jnp.einsum('cmhj,chij->cmhi', vf, later_low)) * k_scale
    value_gradient = jnp.einsum('chlm,clhd->cmhd', causal_mask, gf) + jnp.einsum('cmhi,chij->cmhj', kf, later_low)
    flat = (TOKENS, HEADS * HEAD_DIM)
    query_gradient = query_gradient.astype(bf16).reshape(flat)
    key_gradient = key_gradient.astype(bf16).reshape(flat)
    value_gradient = value_gradient.astype(bf16).reshape(flat)
    inputs_t = inputs.T
    grad_wq = jnp.dot(inputs_t, query_gradient, preferred_element_type=single_precision).astype(bf16)
    grad_wk = jnp.dot(inputs_t, key_gradient, preferred_element_type=single_precision).astype(bf16)
    grad_wv = jnp.dot(inputs_t, value_gradient, preferred_element_type=single_precision).astype(bf16)
    width = HEADS_DEV * HEAD_DIM
    contract = (((1,), (1,)), ((), ()))
    total = jnp.zeros((TOKENS, D), dtype=single_precision)
    for group in range(N_HEAD):
        lo = group * width
        hi = lo + width
        part = lax.dot_general(query_gradient[:, lo:hi], w_query[:, lo:hi], contract, preferred_element_type=single_precision)
        part = part + lax.dot_general(key_gradient[:, lo:hi], w_key[:, lo:hi], contract, preferred_element_type=single_precision)
        part = part + lax.dot_general(value_gradient[:, lo:hi], w_value[:, lo:hi], contract, preferred_element_type=single_precision)
        rounded = lax.optimization_barrier(part.astype(bf16))
        total = total + rounded.astype(single_precision)
    grad_x = total.astype(bf16)
    return attended, grad_wq, grad_wk, grad_wv, grad_x
```

```python
import jax
import jax.numpy as jnp
from jax import lax
from jax.experimental import pallas as pl
from jax.experimental.pallas import tpu as pltpu
from jax.sharding import Mesh, PartitionSpec as P

HEAD_DIM = 128
N = 4
F32 = jnp.float32
BF16 = jnp.bfloat16
NT = (((1,), (1,)), ((), ()))
TN = (((0,), (0,)), ((), ()))


def shift(value, axis, by):
    n = lax.axis_size(axis)
    return lax.ppermute(value, axis, [(i, (i + by) % n) for i in range(n)])


def dot(a, b, dims=(((1,), (0,)), ((), ()))):
    return lax.dot_general(a, b, dims, preferred_element_type=F32)


def shape(*dims, dtype=BF16):
    return jax.ShapeDtypeStruct(dims, dtype)


def grid_call(body, grid, in_specs, out_specs, outs, scratch=(), name=None):
    return pl.pallas_call(
        body,
        out_shape=outs,
        grid_spec=pltpu.PrefetchScalarGridSpec(
            num_scalar_prefetch=1,
            grid=(grid,),
            in_specs=in_specs,
            out_specs=out_specs,
            scratch_shapes=scratch,
        ),
        compiler_params=pltpu.CompilerParams(
            dimension_semantics=("arbitrary",), vmem_limit_bytes=48 << 20
        ),
        name=name,
    )


def project(place, inputs, wq, wk, wv, grad_out):
    rows, model = inputs.shape
    width = wq.shape[1]
    heads = width // HEAD_DIM
    blk = model // (N * N)
    half = blk // 2
    q_scale = HEAD_DIM ** (-0.5)
    k_scale = (rows * N * N) ** (-0.5)

    def body(place, x, a, b, c, g, q_out, k_out, v_out, both, own1, own2, s11, s12, s13, s21, s22, s23, acc):
        i = pl.program_id(0)
        xs = x[...]
        for n, w in enumerate((a, b, c)):
            new = dot(xs, w[...])

            @pl.when(i == 0)
            def _():
                acc[n] = new

            @pl.when(i > 0)
            def _():
                acc[n] = acc[n] + new

        turned = xs.T
        low = place[3] == 0
        mine = jnp.where(low, turned[:half], turned[half:])
        theirs = jnp.where(low, turned[half:], turned[:half])

        @pl.when(i < N)
        def _():
            own1[0, :half] = mine
            own1[0, half:] = theirs

        @pl.when(i % N == 0)
        def _():
            own2[0, :half] = mine
            own2[0, half:] = theirs

        for s, ref in ((1, s11), (2, s12), (3, s13)):

            @pl.when(i // N == s)
            def _():
                ref[0] = mine

        for s, ref in ((1, s21), (2, s22), (3, s23)):

            @pl.when(i % N == s)
            def _():
                ref[0] = mine

        @pl.when(i == N * N - 1)
        def _():
            q = (acc[0] * q_scale).astype(BF16)
            k = (acc[1] * k_scale).astype(BF16)
            v = acc[2].astype(BF16)
            q_out[...] = q
            k_out[...] = k
            v_out[...] = v
            for h in range(heads):
                cols = slice(h * HEAD_DIM, (h + 1) * HEAD_DIM)
                both[0, h] = dot(k[:, cols], v[:, cols], TN).astype(BF16)
                both[1, h] = dot(q[:, cols], g[:, cols], TN).astype(BF16)

    def block(i, place):
        return lax.rem(place[0] + i % N, N) * N + lax.rem(place[1] + i // N, N)

    def first(s):
        return lambda i, place: (jnp.clip(i - N * s, 0, N - 1), 0, 0)

    def second(s):
        return lambda i, place: (jnp.maximum(i + N - s, N) // N - 1, 0, 0)

    whole = pl.BlockSpec((rows, width), lambda i, place: (0, 0))
    return grid_call(
        body,
        N * N,
        [pl.BlockSpec((rows, blk), lambda i, place: (0, block(i, place)))]
        + [pl.BlockSpec((blk, width), lambda i, place: (block(i, place), 0))] * 3
        + [whole],
        [whole] * 3
        + [pl.BlockSpec((2, heads, HEAD_DIM, HEAD_DIM), lambda i, place: (0, 0, 0, 0))]
        + [pl.BlockSpec((1, blk, rows), first(0)), pl.BlockSpec((1, blk, rows), second(0))]
        + [pl.BlockSpec((1, half, rows), first(s)) for s in (1, 2, 3)]
        + [pl.BlockSpec((1, half, rows), second(s)) for s in (1, 2, 3)],
        [shape(rows, width)] * 3
        + [shape(2, heads, HEAD_DIM, HEAD_DIM)]
        + [shape(N, blk, rows)] * 2
        + [shape(N, half, rows)] * 6,
        [pltpu.VMEM((3, rows, width), F32)],
        name="project",
    )(place, inputs, wq, wk, wv, grad_out)


def local_part(place, q, k, v, g):
    rows, width = q.shape

    def body(place, q, k, v, g, att, gq, gk, gv):
        q, k, v, g = q[...], k[...], v[...], g[...]
        keep = lax.broadcasted_iota(jnp.int32, (rows, rows), 0) >= lax.broadcasted_iota(
            jnp.int32, (rows, rows), 1
        )
        causal = jnp.where(keep, dot(q, k, NT), 0.0).astype(BF16)
        back = jnp.where(keep, dot(g, v, NT), 0.0).astype(BF16)
        att[...] = dot(causal, v)
        gq[...] = dot(back, k)
        gk[...] = dot(back, q, TN)
        gv[...] = dot(causal, g, TN)

    head = pl.BlockSpec((rows, HEAD_DIM), lambda h, place: (0, h))
    return grid_call(
        body, width // HEAD_DIM, [head] * 4, [head] * 4, [shape(rows, width, dtype=F32)] * 4, name="local"
    )(place, q, k, v, g)


def finish(place, q, k, v, g, local, state_in, before, after, came):
    rows, width = q.shape
    heads = width // HEAD_DIM
    q_scale = HEAD_DIM ** (-0.5)
    k_scale = (rows * N * N) ** (-0.5)

    def body(place, q, k, v, g, la, lq, lk, lv, state, before, after, c1, c2, c3, att, g1, g2):
        h = pl.program_id(0)
        prior = state[0] + before[0]
        later = after[0]
        for s, ref in ((1, c1), (2, c2), (3, c3)):
            new = ref[0].astype(F32)
            lower = s <= place[0]
            prior = prior + jnp.where(lower, new, 0.0)
            later = later + jnp.where(lower, 0.0, new)
        prior = prior.astype(BF16)
        later = later.astype(BF16)
        q, k, v, g = q[...], k[...], v[...], g[...]
        att[...] = (la[...] + dot(q, prior)).astype(BF16)
        gq = ((lq[...] + dot(g, prior, NT)) * q_scale).astype(BF16)
        gk = ((lk[...] + dot(v, later, NT)) * k_scale).astype(BF16)
        gv = (lv[...] + dot(k, later)).astype(BF16)
        for ref, here in ((g1, h < heads // 2), (g2, h >= heads // 2)):

            @pl.when(here)
            def _():
                ref[:, :HEAD_DIM] = gq
                ref[:, HEAD_DIM : 2 * HEAD_DIM] = gk
                ref[:, 2 * HEAD_DIM :] = gv

    head = pl.BlockSpec((rows, HEAD_DIM), lambda h, place: (0, h))
    mat = pl.BlockSpec((1, HEAD_DIM, HEAD_DIM), lambda h, place: (h, 0, 0))
    last = heads // 2
    return grid_call(
        body,
        heads,
        [head] * 8 + [mat] * 6,
        [
            head,
            pl.BlockSpec((rows, 3 * HEAD_DIM), lambda h, place: (0, jnp.minimum(h, last - 1))),
            pl.BlockSpec((rows, 3 * HEAD_DIM), lambda h, place: (0, jnp.maximum(h, last) - last)),
        ],
        [shape(rows, width)] + [shape(rows, 3 * width // 2)] * 2,
        name="finish",
    )(place, q, k, v, g, *local, state_in, before, after, *came)


def back_project(place, g1, g2, wq, wk, wv, other, received=None):
    rows = g1.shape[0]
    model, width = wq.shape
    blk = model // (2 * N)
    heads = width // HEAD_DIM
    separate = received is not None

    def body(place, g1, g2, a, b, c, *rest):
        i = pl.program_id(0)
        grads = rest[-1]

        @pl.when(i == 0)
        def _():
            for n in range(3):
                for h in range(heads):
                    ref = (g1, g2)[h // (heads // 2)]
                    at = (h % (heads // 2)) * 3 + n
                    grads[n, :, h * HEAD_DIM : (h + 1) * HEAD_DIM] = ref[:, at * HEAD_DIM : (at + 1) * HEAD_DIM]

        total = dot(grads[0], a[...], NT) + dot(grads[1], b[...], NT) + dot(grads[2], c[...], NT)
        if separate:
            near = (total.astype(BF16).astype(F32) + rest[0][0].astype(F32)).astype(BF16)
            for s in range(N):

                @pl.when(i == s)
                def _():
                    rest[1 + s][...] = near
        else:
            rest[0][0] = total.astype(BF16)

    def block(i, place):
        core = 1 - place[3] if other else place[3]
        return lax.rem(place[2] + i, N) * 2 + core

    grad = pl.BlockSpec(g1.shape, lambda i, place: (0, 0))
    stacked = pl.BlockSpec((1, rows, blk), lambda i, place: (i, 0, 0))
    single = pl.BlockSpec((rows, blk), lambda i, place: (0, 0))
    return grid_call(
        body,
        N,
        [grad] * 2
        + [pl.BlockSpec((blk, width), lambda i, place: (block(i, place), 0))] * 3
        + ([stacked] if separate else []),
        [single] * N if separate else stacked,
        [shape(rows, blk)] * N if separate else shape(N, rows, blk),
        [pltpu.VMEM((3, rows, width), BF16)],
        name="back_project",
    )(place, g1, g2, wq, wk, wv, *([received] if separate else []))


def weight_blocks(place, own, mine, theirs, rhs):
    _, blk, rows = own.shape
    half = blk // 2
    cols = rhs[0].shape[1]

    def body(place, own, m1, m2, m3, t1, t2, t3, r0, r1, r2, r3, *outs):
        i = pl.program_id(0)
        total = dot(own[0], r0[...])
        upper = total[:half]
        lower = total[half:]
        for m, t, r in ((m1, t1, r1), (m2, t2, r2), (m3, t3, r3)):
            upper = upper + dot(m[0], r[...])
            lower = lower + dot(t[0], r[...])
        for s in range(N):

            @pl.when(i == s)
            def _():
                outs[s][:half] = upper.astype(BF16)
                outs[s][half:] = lower.astype(BF16)

    full = pl.BlockSpec((1, blk, rows), lambda i, place: (i, 0, 0))
    part = pl.BlockSpec((1, half, rows), lambda i, place: (i, 0, 0))
    grad = pl.BlockSpec((rows, cols), lambda i, place: (0, 0))
    out = pl.BlockSpec((blk, cols), lambda i, place: (0, 0))
    return grid_call(
        body, N, [full] + [part] * 6 + [grad] * 4, [out] * N, [shape(blk, cols)] * N, name="weights"
    )(place, own, *mine, *theirs, *rhs)


def collect(place, first, second):
    blk, cols = first[0].shape
    half = blk // 2
    per = cols // (3 * HEAD_DIM)
    width = 2 * per * HEAD_DIM

    def body(place, *refs):
        outs = refs[2 * N :]
        for n, group in enumerate((refs[:N], refs[N : 2 * N])):
            total = group[0][...].astype(F32)
            for ref in group[1:]:
                total = total + ref[...].astype(F32)
            total = total.astype(BF16)
            for p in range(per):
                for m in range(3):
                    at = (p * 3 + m) * HEAD_DIM
                    to = (n * per + p) * HEAD_DIM
                    outs[m][:, to : to + HEAD_DIM] = total[:, at : at + HEAD_DIM]

    def flipped(i, place):
        return (jnp.where(place[3] == 0, i, 1 - i), 0)

    share = pl.BlockSpec((half, cols), lambda i, place: (i, 0))
    return grid_call(
        body,
        2,
        [share] * (2 * N),
        [pl.BlockSpec((half, width), flipped)] * 3,
        [shape(blk, width)] * 3,
        name="collect",
    )(place, *first, *second)


def after_all(value, *others):
    return lax.optimization_barrier((value, *others))[0]


def shards(inputs, w_query, w_key, w_value, state_in, grad_out):
    y, z = lax.axis_index("y"), lax.axis_index("z")
    place = jnp.stack([y, z, lax.axis_index("x"), lax.axis_index("c")]).astype(jnp.int32)
    q, k, v, both, own1, own2, *sends = project(place, inputs, w_query, w_key, w_value, grad_out)

    got = {s: shift(both, "z", s).astype(F32) for s in (1, 3, 2)}
    total = both.astype(F32) + got[1] + got[2] + got[3]
    before = jnp.zeros_like(state_in)
    after = jnp.zeros_like(state_in)
    for s in (1, 2, 3):
        before = before + jnp.where(s <= z, got[s][0], 0.0)
        after = after + jnp.where(s > z, got[s][1], 0.0)
    out = {s: jnp.where(y + s < N, total[0], total[1]).astype(BF16) for s in (1, 3, 2)}
    came = {s: shift(out[s], "y", s) for s in (1, 3, 2)}
    local = local_part(place, q, k, v, grad_out)

    sends = lax.optimization_barrier((*sends, *out.values()))[:6]
    order = (1, 3, 2)
    mine1 = {s: shift(sends[s - 1], "z", s) for s in order}
    mine2 = {s: shift(sends[s + 2], "y", s) for s in order}
    theirs1 = {s: shift(mine1[s], "c", 1) for s in order}
    theirs2 = {s: shift(mine2[s], "c", 1) for s in order}

    attended, g1, g2 = finish(
        place, q, k, v, grad_out, local, state_in, before, after, [came[s] for s in (1, 2, 3)]
    )
    rhs1 = {s: shift(g1, "z", s) for s in order}
    rhs2 = {s: shift(g2, "y", s) for s in order}
    rhs1[0], rhs2[0] = g1, g2

    far = back_project(place, g1, g2, w_query, w_key, w_value, True)
    near = back_project(place, g1, g2, w_query, w_key, w_value, False, shift(far, "c", 1))
    grad_x = near[0].astype(F32)
    for s in order:
        grad_x = grad_x + shift(near[s], "x", s).astype(F32)
    grad_x = grad_x.astype(BF16)

    def scattered(own, mine, theirs, rhs, axis):
        three = (1, 2, 3)
        blocks = weight_blocks(
            place, own, [mine[s] for s in three], [theirs[s] for s in three], [rhs[s] for s in range(N)]
        )
        return [blocks[0]] + [shift(blocks[s], axis, s) for s in order]

    grads = collect(
        place,
        scattered(own1, mine1, theirs1, rhs1, "y"),
        scattered(own2, mine2, theirs2, rhs2, "z"),
    )
    return (attended, *grads, grad_x)


def solution(mesh):
    fine = Mesh(mesh.devices.reshape(N, N, N, 2), ("y", "z", "x", "c"))
    seq, head = ("y", "z"), ("x", "c")
    in_specs = (P(seq, None), P(None, head), P(None, head), P(None, head), P(head, None, None), P(seq, head))
    out_specs = (P(seq, head),) * 5
    return jax.shard_map(shards, mesh=fine, in_specs=in_specs, out_specs=out_specs, check_vma=False)
```

```python
import jax
import jax.numpy as jnp
from jax import lax
from jax.experimental import pallas as pl
from jax.experimental.pallas import tpu as pltpu
from jax.sharding import Mesh, PartitionSpec as P


HEAD_DIM = 128
N = 4
SPLIT = 7
F32 = jnp.float32
BF16 = jnp.bfloat16
NT = (((1,), (1,)), ((), ()))
TN = (((0,), (0,)), ((), ()))


def shift(value, axis, by):
    n = lax.axis_size(axis)
    return lax.ppermute(value, axis, [(i, (i + by) % n) for i in range(n)])


def dot(a, b, dims=(((1,), (0,)), ((), ()))):
    return lax.dot_general(a, b, dims, preferred_element_type=F32)


def shape(*dims, dtype=BF16):
    return jax.ShapeDtypeStruct(dims, dtype)


def grid_call(body, grid, in_specs, out_specs, outs, scratch=(), mib=16):
    return pl.pallas_call(
        body,
        out_shape=outs,
        grid_spec=pltpu.PrefetchScalarGridSpec(
            num_scalar_prefetch=1,
            grid=(grid,),
            in_specs=in_specs,
            out_specs=out_specs,
            scratch_shapes=scratch,
        ),
        compiler_params=pltpu.CompilerParams(
            dimension_semantics=("arbitrary",), vmem_limit_bytes=mib << 20
        ),
    )


def in_hbm(array):
    return pltpu.with_memory_space_constraint(array, pltpu.HBM)


def whole_call(body, ins, outs, mib=16):
    vmem = pl.BlockSpec(memory_space=pltpu.VMEM)
    smem = pl.BlockSpec(memory_space=pltpu.SMEM)
    return pl.pallas_call(
        body,
        out_shape=outs,
        in_specs=[smem if i.dtype == jnp.int32 else vmem for i in ins],
        out_specs=[vmem] * len(outs),
        compiler_params=pltpu.CompilerParams(vmem_limit_bytes=mib << 20),
    )(*ins)


def project(inputs, wq, wk, wv):
    rows, _ = inputs.shape
    q = (dot(inputs, wq) * HEAD_DIM ** (-0.5)).astype(BF16)
    k = (dot(inputs, wk) * (rows * N * N) ** (-0.5)).astype(BF16)
    return q, k, dot(inputs, wv).astype(BF16)


def block_sums(q, k, v, g):
    heads = q.shape[1] // HEAD_DIM

    def body(q, k, v, g, both):
        for h in range(heads):
            at = slice(h * HEAD_DIM, (h + 1) * HEAD_DIM)
            both[0, h] = dot(k[:, at], v[:, at], TN).astype(BF16)
            both[1, h] = dot(q[:, at], g[:, at], TN).astype(BF16)

    return whole_call(body, (q, k, v, g), [shape(2, heads, HEAD_DIM, HEAD_DIM)])[0]


def turn(place, inputs):
    rows, model = inputs.shape
    blk = model // (N * N)
    half = blk // 2

    def body(place, x, *outs):
        low = place[3] == 0
        for s1 in range(N):
            for s2 in range(N):
                block = lax.rem(place[0] + s2, N) * N + lax.rem(place[1] + s1, N)
                turned = x[:, pl.ds(pl.multiple_of(block * blk, 128), blk)].T
                mine = jnp.where(low, turned[:half], turned[half:])
                theirs = jnp.where(low, turned[half:], turned[:half])
                at1 = slice(s2 * half, (s2 + 1) * half)
                at2 = slice(s1 * half, (s1 + 1) * half)
                outs[s1][at1] = mine
                outs[4 + s2][at2] = mine
                if s1 == 0:
                    outs[8][at1] = theirs
                if s2 == 0:
                    outs[9][at2] = theirs

    whole = pl.BlockSpec((rows, model), lambda i, place: (0, 0))
    piece = pl.BlockSpec((N * half, rows), lambda i, place: (0, 0))
    return grid_call(
        body, 1, [whole], [piece] * 10, [pltpu.HBM((N * half, rows), BF16)] * 10, mib=24
    )(place, in_hbm(inputs))


def local_part(q, k, v, g):
    rows, width = q.shape

    def body(q, k, v, g, att, gq, gk, gv):
        keep = lax.broadcasted_iota(jnp.int32, (rows, rows), 0) >= lax.broadcasted_iota(
            jnp.int32, (rows, rows), 1
        )
        for h in range(0, width, HEAD_DIM):
            at = slice(h, h + HEAD_DIM)
            qh, kh, vh, gh = q[:, at], k[:, at], v[:, at], g[:, at]
            causal = jnp.where(keep, dot(qh, kh, NT), 0.0).astype(BF16)
            back = jnp.where(keep, dot(gh, vh, NT), 0.0).astype(BF16)
            att[:, at] = dot(causal, vh)
            gq[:, at] = dot(back, kh)
            gk[:, at] = dot(back, qh, TN)
            gv[:, at] = dot(causal, gh, TN)

    return whole_call(body, (q, k, v, g), [shape(rows, width, dtype=F32)] * 4)


def row_sums(place, both, got, state_in):
    heads = state_in.shape[0]

    def body(place, both, r1, r2, r3, state, *outs):
        total = both[...].astype(F32)
        prior = state[...]
        later = jnp.zeros_like(prior)
        for s, ref in ((1, r1), (2, r2), (3, r3)):
            new = ref[...].astype(F32)
            total = total + new
            lower = s <= place[1]
            prior = prior + jnp.where(lower, new[0], 0.0)
            later = later + jnp.where(lower, 0.0, new[1])
        for s in (1, 2, 3):
            outs[s - 1][...] = jnp.where(place[0] + s < N, total[0], total[1]).astype(BF16)
        outs[3][...] = prior
        outs[4][...] = later

    mat = (heads, HEAD_DIM, HEAD_DIM)
    return whole_call(body, (place, both, *got, state_in), [shape(*mat)] * 3 + [shape(*mat, dtype=F32)] * 2)


def finish(place, q, k, v, g, local, prior, later, came):
    rows, width = q.shape
    heads = width // HEAD_DIM
    q_scale = HEAD_DIM ** (-0.5)
    k_scale = (rows * N * N) ** (-0.5)

    def body(place, q, k, v, g, la, lq, lk, lv, before, after, c1, c2, c3, att, g1, g2):
        for h in range(heads):
            prior = before[h]
            later = after[h]
            for s, ref in ((1, c1), (2, c2), (3, c3)):
                new = ref[h].astype(F32)
                lower = s <= place[0]
                prior = prior + jnp.where(lower, new, 0.0)
                later = later + jnp.where(lower, 0.0, new)
            prior = prior.astype(BF16)
            later = later.astype(BF16)
            at = slice(h * HEAD_DIM, (h + 1) * HEAD_DIM)
            qh, kh, vh, gh = q[:, at], k[:, at], v[:, at], g[:, at]
            att[:, at] = (la[:, at] + dot(qh, prior)).astype(BF16)
            new = (
                (lq[:, at] + dot(gh, prior, NT)) * q_scale,
                (lk[:, at] + dot(vh, later, NT)) * k_scale,
                lv[:, at] + dot(kh, later),
            )
            for n in range(3):
                t = h * 3 + n
                ref, to = (g1, t) if t < SPLIT else (g2, t - SPLIT)
                ref[:, to * HEAD_DIM : (to + 1) * HEAD_DIM] = new[n].astype(BF16)

    return whole_call(
        body,
        (place, q, k, v, g, *local, prior, later, *came),
        [shape(rows, width), shape(rows, SPLIT * HEAD_DIM), shape(rows, 3 * width - SPLIT * HEAD_DIM)],
    )


def far_project(place, g1, g2, wq, wk, wv):
    rows = g1.shape[0]
    model, width = wq.shape
    blk = model // (2 * N)

    def body(place, g1, g2, a, b, c, out, kept, grads, w, far_sem, near_sem):
        def fetch(i, n, core, to, sem):
            first = (lax.rem(place[2] + i, N) * 2 + core) * blk
            return pltpu.make_async_copy(
                (a, b, c)[n].at[pl.ds(pl.multiple_of(first, 16), blk)],
                to.at[i, :, n * width : (n + 1) * width],
                sem.at[i, n],
            )

        def far(i, n):
            return fetch(i, n, 1 - place[3], w, far_sem)

        def near(i, n):
            return fetch(i, n, place[3], kept, near_sem)

        for i in range(N):
            for n in range(3):
                far(i, n).start()
        for p, ref in enumerate((g1, g2)):
            for at in range(ref.shape[1] // HEAD_DIM):
                t = p * SPLIT + at
                to = (t % 3) * width + t // 3 * HEAD_DIM
                grads[to : to + HEAD_DIM] = ref[:, at * HEAD_DIM : (at + 1) * HEAD_DIM].T
        for i in range(N):
            for n in range(3):
                far(i, n).wait()
            for n in range(3):
                near(i, n).start()
            out[i] = dot(w[i], grads[...]).astype(BF16)
        for i in range(N):
            for n in range(3):
                near(i, n).wait()

    hbm = pl.BlockSpec(memory_space=pltpu.HBM)
    vmem = pl.BlockSpec(memory_space=pltpu.VMEM)
    return pl.pallas_call(
        body,
        out_shape=[shape(N, blk, rows), pltpu.VMEM((N, blk, 3 * width), BF16), shape(3 * width, rows)],
        in_specs=[pl.BlockSpec(memory_space=pltpu.SMEM), vmem, vmem] + [hbm] * 3,
        out_specs=[vmem] * 3,
        scratch_shapes=[
            pltpu.VMEM((N, blk, 3 * width), BF16),
            pltpu.SemaphoreType.DMA((N, 3)),
            pltpu.SemaphoreType.DMA((N, 3)),
        ],
        compiler_params=pltpu.CompilerParams(vmem_limit_bytes=24 << 20),
        name="far",
    )(place, g1, g2, *map(in_hbm, (wq, wk, wv)))


def near_project(kept, grads, received):
    blk = kept.shape[1]
    rows = grads.shape[1]

    def body(kept, grads, received, *outs):
        for s in range(N):
            mine = dot(kept[s], grads[...]).astype(BF16).astype(F32)
            outs[s][...] = (mine + received[s].astype(F32)).astype(BF16)

    return whole_call(body, (kept, grads, received), [shape(blk, rows)] * N)


def total_of(shares):
    blk, rows = shares[0].shape

    def body(a, b, c, d, out):
        total = a[...].astype(F32) + b[...].astype(F32) + c[...].astype(F32) + d[...].astype(F32)
        out[...] = total.astype(BF16).T

    return whole_call(body, shares, [shape(rows, blk)])[0]


def weight_blocks(mine, theirs, rhs):
    half = mine[0].shape[0] // N
    cols = rhs[0].shape[1]

    def body(*refs):
        outs = refs[3 * N :]
        right = jnp.concatenate([r[...] for r in refs[2 * N : 3 * N]], 0)
        for n in range(2):
            left = jnp.concatenate([r[...] for r in refs[n * N : (n + 1) * N]], 1)
            total = dot(left, right).astype(BF16)
            for s in range(N):
                outs[s][n * half : (n + 1) * half] = total[s * half : (s + 1) * half]

    return whole_call(body, (*mine, *theirs, *rhs), [shape(2 * half, cols)] * N)


def collect(place, start, shares, held, width):
    blk, cols = shares[0].shape
    half = blk // 2
    count = cols // HEAD_DIM
    heads = [[t // 3 for t in range(start, start + count) if t % 3 == m] for m in range(3)]

    def body(place, *refs):
        outs = refs[-3:]
        total = refs[0][...].astype(F32)
        for ref in refs[1:N]:
            total = total + ref[...].astype(F32)
        total = total.astype(BF16)
        for at in range(count):
            m, h = (start + at) % 3, (start + at) // 3
            to = (h - heads[m][0]) * HEAD_DIM
            outs[m][:, to : to + HEAD_DIM] = total[:, at * HEAD_DIM : (at + 1) * HEAD_DIM]

    def spec(those):
        return pl.BlockSpec(
            (half, len(those) * HEAD_DIM),
            lambda i, place: (jnp.where(place[3] == 0, i, 1 - i), those[0] // len(those)),
        )

    share = pl.BlockSpec((half, cols), lambda i, place: (i, 0))
    return pl.pallas_call(
        body,
        out_shape=[shape(blk, width)] * 3,
        grid_spec=pltpu.PrefetchScalarGridSpec(
            num_scalar_prefetch=1,
            grid=(2,),
            in_specs=[share] * N + [pl.BlockSpec(memory_space=pl.ANY)] * len(held),
            out_specs=[spec(those) for those in heads],
        ),
        input_output_aliases={1 + N + m: m for m in range(len(held))},
        compiler_params=pltpu.CompilerParams(
            dimension_semantics=("arbitrary",), vmem_limit_bytes=8 << 20
        ),
        name="collect",
    )(place, *shares, *held)


def shards(inputs, w_query, w_key, w_value, state_in, grad_out):
    width = w_query.shape[1]
    order = (1, 3, 2)
    three = (1, 2, 3)

    place = jnp.stack([lax.axis_index(a) for a in ("y", "z", "x", "c")]).astype(jnp.int32)
    q, k, v = project(inputs, w_query, w_key, w_value)
    both = block_sums(q, k, v, grad_out)
    got = {s: shift(both, "z", s) for s in order}

    pieces = turn(place, inputs)
    local = local_part(q, k, v, grad_out)
    *out, prior, later = row_sums(place, both, [got[s] for s in three], state_in)
    came = {s: shift(out[s - 1], "y", s) for s in order}

    mine1 = {s: shift(pieces[s], "z", s) for s in order}
    mine2 = {s: shift(pieces[4 + s], "y", s) for s in order}
    theirs1 = {s: shift(mine1[s], "c", 1) for s in order}
    theirs2 = {s: shift(mine2[s], "c", 1) for s in order}
    mine1[0], mine2[0], theirs1[0], theirs2[0] = pieces[0], pieces[4], pieces[8], pieces[9]

    attended, g1, g2 = finish(
        place, q, k, v, grad_out, local, prior, later, [came[s] for s in three]
    )
    rhs1 = {s: shift(g1, "z", s) for s in order}
    rhs2 = {s: shift(g2, "y", s) for s in order}
    rhs1[0], rhs2[0] = g1, g2

    far, kept, turned = far_project(place, g1, g2, w_query, w_key, w_value)
    far = shift(far, "c", 1)
    near = near_project(kept, turned, far)
    across = {s: shift(near[s], "x", s) for s in order}
    grad_x = total_of((near[0], *across.values()))

    def scattered(mine, theirs, rhs, axis):
        blocks = weight_blocks(*([a[s] for s in range(N)] for a in (mine, theirs, rhs)))
        return [blocks[0]] + [shift(blocks[s], axis, s) for s in order]

    first = scattered(mine1, theirs1, rhs1, "y")
    second = scattered(mine2, theirs2, rhs2, "z")
    grads = collect(place, 0, first, (), width)
    grads = collect(place, SPLIT, second, grads, width)
    return (attended, *grads, grad_x)


def solution(mesh):
    fine = Mesh(mesh.devices.reshape(N, N, N, 2), ("y", "z", "x", "c"))
    seq, head = ("y", "z"), ("x", "c")
    in_specs = (P(seq, None), P(None, head), P(None, head), P(None, head), P(head, None, None), P(seq, head))
    out_specs = (P(seq, head),) * 5

    return jax.shard_map(shards, mesh=fine, in_specs=in_specs, out_specs=out_specs, check_vma=False)
```

```python
import jax
import jax.numpy as jnp
from jax import lax
from jax.experimental import pallas as pl
from jax.experimental.pallas import tpu as pltpu
from jax.sharding import Mesh, PartitionSpec as P


HEAD_DIM = 128
N = 4
SPLIT = 7
F32 = jnp.float32
BF16 = jnp.bfloat16
NT = (((1,), (1,)), ((), ()))
TN = (((0,), (0,)), ((), ()))


def shift(value, axis, by):
    n = lax.axis_size(axis)
    return lax.ppermute(value, axis, [(i, (i + by) % n) for i in range(n)])


def dot(a, b, dims=(((1,), (0,)), ((), ()))):
    return lax.dot_general(a, b, dims, preferred_element_type=F32)


def shape(*dims, dtype=BF16):
    return jax.ShapeDtypeStruct(dims, dtype)


def in_hbm(array):
    return pltpu.with_memory_space_constraint(array, pltpu.HBM)


def whole_call(body, ins, outs, mib=16):
    vmem = pl.BlockSpec(memory_space=pltpu.VMEM)
    smem = pl.BlockSpec(memory_space=pltpu.SMEM)
    return pl.pallas_call(
        body,
        out_shape=outs,
        in_specs=[smem if i.dtype == jnp.int32 else vmem for i in ins],
        out_specs=[vmem] * len(outs),
        compiler_params=pltpu.CompilerParams(vmem_limit_bytes=mib << 20),
    )(*ins)


def project(inputs, wq, wk, wv):
    rows, _ = inputs.shape
    q = (dot(inputs, wq) * HEAD_DIM ** (-0.5)).astype(BF16)
    k = (dot(inputs, wk) * (rows * N * N) ** (-0.5)).astype(BF16)
    return q, k, dot(inputs, wv).astype(BF16)


def block_sums(q, k, v, g):
    heads = q.shape[1] // HEAD_DIM

    def body(q, k, v, g, both):
        for h in range(heads):
            at = slice(h * HEAD_DIM, (h + 1) * HEAD_DIM)
            both[0, h] = dot(k[:, at], v[:, at], TN).astype(BF16)
            both[1, h] = dot(q[:, at], g[:, at], TN).astype(BF16)

    return whole_call(body, (q, k, v, g), [shape(2, heads, HEAD_DIM, HEAD_DIM)])[0]


def turn(place, inputs):
    rows, model = inputs.shape
    blk = model // (N * N)
    half = blk // 2
    part = model // N

    def body(place, x_hbm, *refs):
        outs, (x, pieces, x_sem, out_sem) = refs[:10], refs[10:]

        def lanes(s2):
            return pl.ds(pl.multiple_of(lax.rem(place[0] + s2, N) * part, 128), part)

        def load(s2):
            return pltpu.make_async_copy(x_hbm.at[:, lanes(s2)], x.at[:, lanes(s2)], x_sem.at[s2])

        def store(p):
            return pltpu.make_async_copy(pieces.at[p], outs[p], out_sem.at[p])

        for s2 in range(N):
            load(s2).start()
        low = place[3] == 0
        for s2 in range(N):
            load(s2).wait()
            for s1 in range(N):
                block = lax.rem(place[0] + s2, N) * N + lax.rem(place[1] + s1, N)
                turned = x[:, pl.ds(pl.multiple_of(block * blk, 128), blk)].T
                mine = jnp.where(low, turned[:half], turned[half:])
                theirs = jnp.where(low, turned[half:], turned[:half])
                at1 = slice(s2 * half, (s2 + 1) * half)
                at2 = slice(s1 * half, (s1 + 1) * half)
                pieces[s1, at1] = mine
                pieces[4 + s2, at2] = mine
                if s1 == 0:
                    pieces[8, at1] = theirs
                if s2 == 0:
                    pieces[9, at2] = theirs
            store(4 + s2).start()
        for p in (0, 1, 2, 3, 8, 9):
            store(p).start()
        for p in range(10):
            store(p).wait()

    hbm = pl.BlockSpec(memory_space=pltpu.HBM)
    piece = (N * half, rows)
    return pl.pallas_call(
        body,
        out_shape=[pltpu.HBM(piece, BF16)] * 10,
        in_specs=[pl.BlockSpec(memory_space=pltpu.SMEM), hbm],
        out_specs=[hbm] * 10,
        scratch_shapes=[
            pltpu.VMEM(inputs.shape, BF16),
            pltpu.VMEM((10, *piece), BF16),
            pltpu.SemaphoreType.DMA((N,)),
            pltpu.SemaphoreType.DMA((10,)),
        ],
        compiler_params=pltpu.CompilerParams(vmem_limit_bytes=16 << 20),
        name="turn",
    )(place, in_hbm(inputs))


def local_part(q, k, v, g):
    rows, width = q.shape

    def body(q, k, v, g, att, gq, gk, gv):
        keep = lax.broadcasted_iota(jnp.int32, (rows, rows), 0) >= lax.broadcasted_iota(
            jnp.int32, (rows, rows), 1
        )
        for h in range(0, width, HEAD_DIM):
            at = slice(h, h + HEAD_DIM)
            qh, kh, vh, gh = q[:, at], k[:, at], v[:, at], g[:, at]
            causal = jnp.where(keep, dot(qh, kh, NT), 0.0).astype(BF16)
            back = jnp.where(keep, dot(gh, vh, NT), 0.0).astype(BF16)
            att[:, at] = dot(causal, vh)
            gq[:, at] = dot(back, kh)
            gk[:, at] = dot(back, qh, TN)
            gv[:, at] = dot(causal, gh, TN)

    return whole_call(body, (q, k, v, g), [shape(rows, width, dtype=F32)] * 4)


def row_sums(place, both, got, state_in):
    heads = state_in.shape[0]

    def body(place, both, r1, r2, r3, state, *outs):
        total = both[...].astype(F32)
        prior = state[...]
        later = jnp.zeros_like(prior)
        for s, ref in ((1, r1), (2, r2), (3, r3)):
            new = ref[...].astype(F32)
            total = total + new
            lower = s <= place[1]
            prior = prior + jnp.where(lower, new[0], 0.0)
            later = later + jnp.where(lower, 0.0, new[1])
        for s in (1, 2, 3):
            outs[s - 1][...] = jnp.where(place[0] + s < N, total[0], total[1]).astype(BF16)
        outs[3][...] = prior
        outs[4][...] = later

    mat = (heads, HEAD_DIM, HEAD_DIM)
    return whole_call(body, (place, both, *got, state_in), [shape(*mat)] * 3 + [shape(*mat, dtype=F32)] * 2)


def finish(place, q, k, v, g, local, prior, later, came):
    rows, width = q.shape
    heads = width // HEAD_DIM
    q_scale = HEAD_DIM ** (-0.5)
    k_scale = (rows * N * N) ** (-0.5)

    def body(place, q, k, v, g, la, lq, lk, lv, before, after, c1, c2, c3, att, g1, g2):
        for h in range(heads):
            prior = before[h]
            later = after[h]
            for s, ref in ((1, c1), (2, c2), (3, c3)):
                new = ref[h].astype(F32)
                lower = s <= place[0]
                prior = prior + jnp.where(lower, new, 0.0)
                later = later + jnp.where(lower, 0.0, new)
            prior = prior.astype(BF16)
            later = later.astype(BF16)
            at = slice(h * HEAD_DIM, (h + 1) * HEAD_DIM)
            qh, kh, vh, gh = q[:, at], k[:, at], v[:, at], g[:, at]
            att[:, at] = (la[:, at] + dot(qh, prior)).astype(BF16)
            new = (
                (lq[:, at] + dot(gh, prior, NT)) * q_scale,
                (lk[:, at] + dot(vh, later, NT)) * k_scale,
                lv[:, at] + dot(kh, later),
            )
            for n in range(3):
                t = h * 3 + n
                ref, to = (g1, t) if t < SPLIT else (g2, t - SPLIT)
                ref[:, to * HEAD_DIM : (to + 1) * HEAD_DIM] = new[n].astype(BF16)

    return whole_call(
        body,
        (place, q, k, v, g, *local, prior, later, *came),
        [shape(rows, width), shape(rows, SPLIT * HEAD_DIM), shape(rows, 3 * width - SPLIT * HEAD_DIM)],
    )


def far_project(place, g1, g2, wq, wk, wv):
    rows = g1.shape[0]
    model, width = wq.shape
    blk = model // (2 * N)

    def body(place, g1, g2, a, b, c, out, kept, grads, w, far_sem, near_sem):
        def fetch(i, n, core, to, sem):
            first = (lax.rem(place[2] + i, N) * 2 + core) * blk
            return pltpu.make_async_copy(
                (a, b, c)[n].at[pl.ds(pl.multiple_of(first, 16), blk)],
                to.at[i, :, n * width : (n + 1) * width],
                sem.at[i, n],
            )

        def far(i, n):
            return fetch(i, n, 1 - place[3], w, far_sem)

        def near(i, n):
            return fetch(i, n, place[3], kept, near_sem)

        for i in range(N):
            for n in range(3):
                far(i, n).start()
        for p, ref in enumerate((g1, g2)):
            for at in range(ref.shape[1] // HEAD_DIM):
                t = p * SPLIT + at
                to = (t % 3) * width + t // 3 * HEAD_DIM
                grads[to : to + HEAD_DIM] = ref[:, at * HEAD_DIM : (at + 1) * HEAD_DIM].T
        for i in range(N):
            for n in range(3):
                far(i, n).wait()
            for n in range(3):
                near(i, n).start()
            out[i] = dot(w[i], grads[...]).astype(BF16)
        for i in range(N):
            for n in range(3):
                near(i, n).wait()

    hbm = pl.BlockSpec(memory_space=pltpu.HBM)
    vmem = pl.BlockSpec(memory_space=pltpu.VMEM)
    return pl.pallas_call(
        body,
        out_shape=[shape(N, blk, rows), pltpu.VMEM((N, blk, 3 * width), BF16), shape(3 * width, rows)],
        in_specs=[pl.BlockSpec(memory_space=pltpu.SMEM), vmem, vmem] + [hbm] * 3,
        out_specs=[vmem] * 3,
        scratch_shapes=[
            pltpu.VMEM((N, blk, 3 * width), BF16),
            pltpu.SemaphoreType.DMA((N, 3)),
            pltpu.SemaphoreType.DMA((N, 3)),
        ],
        compiler_params=pltpu.CompilerParams(vmem_limit_bytes=24 << 20),
        name="far",
    )(place, g1, g2, *map(in_hbm, (wq, wk, wv)))


def near_project(kept, grads, received):
    blk = kept.shape[1]
    rows = grads.shape[1]

    def body(kept, grads, received, *outs):
        for s in range(N):
            mine = dot(kept[s], grads[...]).astype(BF16).astype(F32)
            outs[s][...] = (mine + received[s].astype(F32)).astype(BF16)

    return whole_call(body, (kept, grads, received), [shape(blk, rows)] * N)


def weight_blocks(mine, theirs, rhs):
    half = mine[0].shape[0] // N
    cols = rhs[0].shape[1]

    def body(*refs):
        outs = refs[3 * N :]
        right = jnp.concatenate([r[...] for r in refs[2 * N : 3 * N]], 0)
        for n in range(2):
            left = jnp.concatenate([r[...] for r in refs[n * N : (n + 1) * N]], 1)
            total = dot(left, right).astype(BF16)
            for s in range(N):
                outs[s][n * half : (n + 1) * half] = total[s * half : (s + 1) * half]

    return whole_call(body, (*mine, *theirs, *rhs), [shape(2 * half, cols)] * N)


def collect(place, across, first, second, width):
    rows = across[0].shape[1]
    model = across[0].shape[0]
    blk = first[0].shape[0]
    half = blk // 2

    def body(place, *refs):
        grad_x, *outs = refs[3 * N :]

        def total(which, rows=slice(None)):
            value = refs[which * N][rows].astype(F32)
            for ref in refs[which * N + 1 : which * N + N]:
                value = value + ref[rows].astype(F32)
            return value.astype(BF16)

        grad_x[...] = total(0).T
        for n in range(2):
            core = place[3] if n == 0 else 1 - place[3]
            to = pl.ds(pl.multiple_of(core * half, 64), half)
            for which, start in ((1, 0), (2, SPLIT)):
                value = total(which, slice(n * half, (n + 1) * half))
                for at in range(value.shape[1] // HEAD_DIM):
                    h, m = divmod(start + at, 3)
                    outs[m][to, h * HEAD_DIM : (h + 1) * HEAD_DIM] = value[:, at * HEAD_DIM : (at + 1) * HEAD_DIM]

    return whole_call(body, (place, *across, *first, *second), [shape(rows, model)] + [shape(blk, width)] * 3)


def shards(inputs, w_query, w_key, w_value, state_in, grad_out):
    width = w_query.shape[1]
    order = (1, 3, 2)
    three = (1, 2, 3)

    place = jnp.stack([lax.axis_index(a) for a in ("y", "z", "x", "c")]).astype(jnp.int32)
    pieces = turn(place, inputs)
    q, k, v = project(inputs, w_query, w_key, w_value)
    both = block_sums(q, k, v, grad_out)
    got = {s: shift(both, "z", s) for s in order}

    local = local_part(q, k, v, grad_out)
    *out, prior, later = row_sums(place, both, [got[s] for s in three], state_in)
    came = {s: shift(out[s - 1], "y", s) for s in order}

    mine1 = {s: shift(pieces[s], "z", s) for s in order}
    mine2 = {s: shift(pieces[4 + s], "y", s) for s in order}
    theirs1 = {s: shift(mine1[s], "c", 1) for s in order}
    theirs2 = {s: shift(mine2[s], "c", 1) for s in order}
    mine1[0], mine2[0], theirs1[0], theirs2[0] = pieces[0], pieces[4], pieces[8], pieces[9]

    attended, g1, g2 = finish(
        place, q, k, v, grad_out, local, prior, later, [came[s] for s in three]
    )
    rhs1 = {s: shift(g1, "z", s) for s in order}
    rhs2 = {s: shift(g2, "y", s) for s in order}
    rhs1[0], rhs2[0] = g1, g2

    far, kept, turned = far_project(place, g1, g2, w_query, w_key, w_value)
    far = shift(far, "c", 1)
    near = near_project(kept, turned, far)
    across = {s: shift(near[s], "x", s) for s in order}

    def scattered(mine, theirs, rhs, axis):
        blocks = weight_blocks(*([a[s] for s in range(N)] for a in (mine, theirs, rhs)))
        return [blocks[0]] + [shift(blocks[s], axis, s) for s in order]

    first = scattered(mine1, theirs1, rhs1, "y")
    second = scattered(mine2, theirs2, rhs2, "z")
    grad_x, *grads = collect(place, (near[0], *across.values()), first, second, width)
    return (attended, *grads, grad_x)


def solution(mesh):
    fine = Mesh(mesh.devices.reshape(N, N, N, 2), ("y", "z", "x", "c"))
    seq, head = ("y", "z"), ("x", "c")
    in_specs = (P(seq, None), P(None, head), P(None, head), P(None, head), P(head, None, None), P(seq, head))
    out_specs = (P(seq, head),) * 5

    return jax.shard_map(shards, mesh=fine, in_specs=in_specs, out_specs=out_specs, check_vma=False)
```

```python
import jax
import jax.numpy as jnp
from jax import lax
from jax.experimental import pallas as pl
from jax.experimental.pallas import tpu as pltpu
from jax.sharding import Mesh, PartitionSpec as P


HEAD_DIM = 128
N = 4
SPLIT = 7
F32 = jnp.float32
BF16 = jnp.bfloat16
NT = (((1,), (1,)), ((), ()))
TN = (((0,), (0,)), ((), ()))


def shift(value, axis, by):
    n = lax.axis_size(axis)
    return lax.ppermute(value, axis, [(i, (i + by) % n) for i in range(n)])


def dot(a, b, dims=(((1,), (0,)), ((), ()))):
    return lax.dot_general(a, b, dims, preferred_element_type=F32)


def shape(*dims, dtype=BF16):
    return jax.ShapeDtypeStruct(dims, dtype)


def in_hbm(array):
    return pltpu.with_memory_space_constraint(array, pltpu.HBM)


def whole_call(body, ins, outs, mib=16):
    vmem = pl.BlockSpec(memory_space=pltpu.VMEM)
    smem = pl.BlockSpec(memory_space=pltpu.SMEM)
    return pl.pallas_call(
        body,
        out_shape=outs,
        in_specs=[smem if i.dtype == jnp.int32 else vmem for i in ins],
        out_specs=[vmem] * len(outs),
        compiler_params=pltpu.CompilerParams(vmem_limit_bytes=mib << 20),
    )(*ins)


def project(inputs, wq, wk, wv):
    rows, _ = inputs.shape
    q = (dot(inputs, wq) * HEAD_DIM ** (-0.5)).astype(BF16)
    k = (dot(inputs, wk) * (rows * N * N) ** (-0.5)).astype(BF16)
    return q, k, dot(inputs, wv).astype(BF16)


def block_sums(q, k, v, g):
    heads = q.shape[1] // HEAD_DIM

    def body(q, k, v, g, both):
        for h in range(heads):
            at = slice(h * HEAD_DIM, (h + 1) * HEAD_DIM)
            both[0, h] = dot(k[:, at], v[:, at], TN).astype(BF16)
            both[1, h] = dot(q[:, at], g[:, at], TN).astype(BF16)

    return whole_call(body, (q, k, v, g), [shape(2, heads, HEAD_DIM, HEAD_DIM)])[0]


def turn(place, inputs):
    rows, model = inputs.shape
    blk = model // (N * N)
    half = blk // 2
    part = model // N

    def body(place, x_hbm, *refs):
        outs, (x, pieces, x_sem, out_sem) = refs[:10], refs[10:]

        def lanes(s2):
            return pl.ds(pl.multiple_of(lax.rem(place[0] + s2, N) * part, 128), part)

        def load(s2):
            return pltpu.make_async_copy(x_hbm.at[:, lanes(s2)], x.at[:, lanes(s2)], x_sem.at[s2])

        def store(p):
            source = pieces.at[p]
            if p == 2:
                source = pieces.at[p, pl.ds(pl.multiple_of(lax.rem(place[2], 2) * blk, 128), blk)]
            return pltpu.make_async_copy(source, outs[p], out_sem.at[p])

        for s2 in range(N):
            load(s2).start()
        low = place[3] == 0
        for s2 in range(N):
            load(s2).wait()
            for s1 in range(N):
                block = lax.rem(place[0] + s2, N) * N + lax.rem(place[1] + s1, N)
                turned = x[:, pl.ds(pl.multiple_of(block * blk, 128), blk)].T
                mine = jnp.where(low, turned[:half], turned[half:])
                theirs = jnp.where(low, turned[half:], turned[:half])
                at1 = slice(s2 * half, (s2 + 1) * half)
                at2 = slice(s1 * half, (s1 + 1) * half)
                pieces[s1, at1] = mine
                pieces[4 + s2, at2] = mine
                if s1 == 0:
                    pieces[8, at1] = theirs
                if s2 == 0:
                    pieces[9, at2] = theirs
            store(4 + s2).start()
        for p in (0, 1, 2, 3, 8, 9):
            store(p).start()
        for p in range(10):
            store(p).wait()

    hbm = pl.BlockSpec(memory_space=pltpu.HBM)
    piece = (N * half, rows)
    return pl.pallas_call(
        body,
        out_shape=[pltpu.HBM((blk, rows) if p == 2 else piece, BF16) for p in range(10)],
        in_specs=[pl.BlockSpec(memory_space=pltpu.SMEM), hbm],
        out_specs=[hbm] * 10,
        scratch_shapes=[
            pltpu.VMEM(inputs.shape, BF16),
            pltpu.VMEM((10, *piece), BF16),
            pltpu.SemaphoreType.DMA((N,)),
            pltpu.SemaphoreType.DMA((10,)),
        ],
        compiler_params=pltpu.CompilerParams(vmem_limit_bytes=16 << 20),
        name="turn",
    )(place, in_hbm(inputs))


def local_part(q, k, v, g):
    rows, width = q.shape

    def body(q, k, v, g, att, gq, gk, gv):
        keep = lax.broadcasted_iota(jnp.int32, (rows, rows), 0) >= lax.broadcasted_iota(
            jnp.int32, (rows, rows), 1
        )
        for h in range(0, width, HEAD_DIM):
            at = slice(h, h + HEAD_DIM)
            qh, kh, vh, gh = q[:, at], k[:, at], v[:, at], g[:, at]
            causal = jnp.where(keep, dot(qh, kh, NT), 0.0).astype(BF16)
            back = jnp.where(keep, dot(gh, vh, NT), 0.0).astype(BF16)
            att[:, at] = dot(causal, vh)
            gq[:, at] = dot(back, kh)
            gk[:, at] = dot(back, qh, TN)
            gv[:, at] = dot(causal, gh, TN)

    return whole_call(body, (q, k, v, g), [shape(rows, width, dtype=F32)] * 4)


def row_sums(place, both, got, state_in):
    heads = state_in.shape[0]

    def body(place, both, r1, r2, r3, state, *outs):
        total = both[...].astype(F32)
        prior = state[...]
        later = jnp.zeros_like(prior)
        for s, ref in ((1, r1), (2, r2), (3, r3)):
            new = ref[...].astype(F32)
            total = total + new
            lower = s <= place[1]
            prior = prior + jnp.where(lower, new[0], 0.0)
            later = later + jnp.where(lower, 0.0, new[1])
        for s in (1, 2, 3):
            outs[s - 1][...] = jnp.where(place[0] + s < N, total[0], total[1]).astype(BF16)
        outs[3][...] = prior
        outs[4][...] = later

    mat = (heads, HEAD_DIM, HEAD_DIM)
    return whole_call(body, (place, both, *got, state_in), [shape(*mat)] * 3 + [shape(*mat, dtype=F32)] * 2)


def finish(place, q, k, v, g, local, prior, later, came):
    rows, width = q.shape
    heads = width // HEAD_DIM
    q_scale = HEAD_DIM ** (-0.5)
    k_scale = (rows * N * N) ** (-0.5)

    def body(place, q, k, v, g, la, lq, lk, lv, before, after, c1, c2, c3, att, g1, g2):
        for h in range(heads):
            prior = before[h]
            later = after[h]
            for s, ref in ((1, c1), (2, c2), (3, c3)):
                new = ref[h].astype(F32)
                lower = s <= place[0]
                prior = prior + jnp.where(lower, new, 0.0)
                later = later + jnp.where(lower, 0.0, new)
            prior = prior.astype(BF16)
            later = later.astype(BF16)
            at = slice(h * HEAD_DIM, (h + 1) * HEAD_DIM)
            qh, kh, vh, gh = q[:, at], k[:, at], v[:, at], g[:, at]
            att[:, at] = (la[:, at] + dot(qh, prior)).astype(BF16)
            new = (
                (lq[:, at] + dot(gh, prior, NT)) * q_scale,
                (lk[:, at] + dot(vh, later, NT)) * k_scale,
                lv[:, at] + dot(kh, later),
            )
            for n in range(3):
                t = h * 3 + n
                ref, to = (g1, t) if t < SPLIT else (g2, t - SPLIT)
                ref[:, to * HEAD_DIM : (to + 1) * HEAD_DIM] = new[n].astype(BF16)

    return whole_call(
        body,
        (place, q, k, v, g, *local, prior, later, *came),
        [shape(rows, width), shape(rows, SPLIT * HEAD_DIM), shape(rows, 3 * width - SPLIT * HEAD_DIM)],
    )


def far_project(place, g1, g2, wq, wk, wv):
    rows = g1.shape[0]
    model, width = wq.shape
    blk = model // (2 * N)

    def body(place, g1, g2, a, b, c, out, kept, grads, w, far_sem, near_sem):
        def fetch(i, n, core, to, sem):
            first = (lax.rem(place[2] + i, N) * 2 + core) * blk
            return pltpu.make_async_copy(
                (a, b, c)[n].at[pl.ds(pl.multiple_of(first, 16), blk)],
                to.at[i, :, n * width : (n + 1) * width],
                sem.at[i, n],
            )

        def far(i, n):
            return fetch(i, n, 1 - place[3], w, far_sem)

        def near(i, n):
            return fetch(i, n, place[3], kept, near_sem)

        for i in range(N):
            for n in range(3):
                far(i, n).start()
        for p, ref in enumerate((g1, g2)):
            for at in range(ref.shape[1] // HEAD_DIM):
                t = p * SPLIT + at
                to = (t % 3) * width + t // 3 * HEAD_DIM
                grads[to : to + HEAD_DIM] = ref[:, at * HEAD_DIM : (at + 1) * HEAD_DIM].T
        for i in range(N):
            for n in range(3):
                far(i, n).wait()
            for n in range(3):
                near(i, n).start()
            out[i] = dot(w[i], grads[...]).astype(BF16)
        for i in range(N):
            for n in range(3):
                near(i, n).wait()

    hbm = pl.BlockSpec(memory_space=pltpu.HBM)
    vmem = pl.BlockSpec(memory_space=pltpu.VMEM)
    return pl.pallas_call(
        body,
        out_shape=[shape(N, blk, rows), pltpu.VMEM((N, blk, 3 * width), BF16), shape(3 * width, rows)],
        in_specs=[pl.BlockSpec(memory_space=pltpu.SMEM), vmem, vmem] + [hbm] * 3,
        out_specs=[vmem] * 3,
        scratch_shapes=[
            pltpu.VMEM((N, blk, 3 * width), BF16),
            pltpu.SemaphoreType.DMA((N, 3)),
            pltpu.SemaphoreType.DMA((N, 3)),
        ],
        compiler_params=pltpu.CompilerParams(vmem_limit_bytes=24 << 20),
        name="far",
    )(place, g1, g2, *map(in_hbm, (wq, wk, wv)))


def near_project(kept, grads, received):
    blk = kept.shape[1]
    rows = grads.shape[1]

    def body(kept, grads, received, *outs):
        for s in range(N):
            mine = dot(kept[s], grads[...]).astype(BF16).astype(F32)
            outs[s][...] = (mine + received[s].astype(F32)).astype(BF16)

    return whole_call(body, (kept, grads, received), [shape(blk, rows)] * N)


def weight_blocks(place, mine, theirs, rhs):
    groups = [[p if isinstance(p, tuple) else (p,) for p in group] for group in (mine, theirs)]
    half = mine[0].shape[0] // N
    cols = rhs[0].shape[1]

    def body(place, *refs):
        refs = list(refs)
        even = lax.rem(place[2], 2) == 0

        def take(pieces):
            values = [refs.pop(0)[...] for _ in pieces]
            if len(values) == 1:
                return values[0]
            a, b = values
            return jnp.concatenate([jnp.where(even, a, b), jnp.where(even, b, a)], 0)

        lefts = [jnp.concatenate([take(pieces) for pieces in group], 1) for group in groups]
        right = jnp.concatenate([refs.pop(0)[...] for _ in range(N)], 0)
        for n in range(2):
            total = dot(lefts[n], right).astype(BF16)
            for s in range(N):
                refs[s][n * half : (n + 1) * half] = total[s * half : (s + 1) * half]

    flat = [a for group in groups for pieces in group for a in pieces]
    return whole_call(body, (place, *flat, *rhs), [shape(2 * half, cols)] * N)


def collect(place, across, first, second, width):
    rows = across[0].shape[1]
    model = across[0].shape[0]
    blk = first[0].shape[0]
    half = blk // 2

    def body(place, *refs):
        grad_x, *outs = refs[3 * N :]

        def total(which, rows=slice(None)):
            value = refs[which * N][rows].astype(F32)
            for ref in refs[which * N + 1 : which * N + N]:
                value = value + ref[rows].astype(F32)
            return value.astype(BF16)

        grad_x[...] = total(0).T
        for n in range(2):
            core = place[3] if n == 0 else 1 - place[3]
            to = pl.ds(pl.multiple_of(core * half, 64), half)
            for which, start in ((1, 0), (2, SPLIT)):
                value = total(which, slice(n * half, (n + 1) * half))
                for at in range(value.shape[1] // HEAD_DIM):
                    h, m = divmod(start + at, 3)
                    outs[m][to, h * HEAD_DIM : (h + 1) * HEAD_DIM] = value[:, at * HEAD_DIM : (at + 1) * HEAD_DIM]

    return whole_call(body, (place, *across, *first, *second), [shape(rows, model)] + [shape(blk, width)] * 3)


def shards(inputs, w_query, w_key, w_value, state_in, grad_out):
    width = w_query.shape[1]
    order = (1, 3, 2)
    three = (1, 2, 3)

    place = jnp.stack([lax.axis_index(a) for a in ("y", "z", "x", "c")]).astype(jnp.int32)
    pieces = turn(place, inputs)
    q, k, v = project(inputs, w_query, w_key, w_value)
    both = block_sums(q, k, v, grad_out)
    got = {s: shift(both, "z", s) for s in order}

    local = local_part(q, k, v, grad_out)
    *out, prior, later = row_sums(place, both, [got[s] for s in three], state_in)
    came = {s: shift(out[s - 1], "y", s) for s in order}

    mine1 = {s: shift(pieces[s], "z", s) for s in order}
    mine2 = {s: shift(pieces[4 + s], "y", s) for s in order}
    other = lax.ppermute(mine1[2], "x", [(i, i ^ 1) for i in range(N)])
    theirs1 = {s: shift(mine1[s], "c", 1) for s in order}
    mine1[2], theirs1[2] = (mine1[2], other), (theirs1[2], shift(other, "c", 1))
    theirs2 = {s: shift(mine2[s], "c", 1) for s in order}
    mine1[0], mine2[0], theirs1[0], theirs2[0] = pieces[0], pieces[4], pieces[8], pieces[9]

    attended, g1, g2 = finish(
        place, q, k, v, grad_out, local, prior, later, [came[s] for s in three]
    )
    rhs1 = {s: shift(g1, "z", s) for s in order}
    rhs2 = {s: shift(g2, "y", s) for s in order}
    rhs1[0], rhs2[0] = g1, g2

    far, kept, turned = far_project(place, g1, g2, w_query, w_key, w_value)
    far = shift(far, "c", 1)
    near = near_project(kept, turned, far)
    across = {s: shift(near[s], "x", s) for s in order}

    def scattered(mine, theirs, rhs, axis):
        blocks = weight_blocks(place, *([a[s] for s in range(N)] for a in (mine, theirs, rhs)))
        return [blocks[0]] + [shift(blocks[s], axis, s) for s in order]

    first = scattered(mine1, theirs1, rhs1, "y")
    second = scattered(mine2, theirs2, rhs2, "z")
    grad_x, *grads = collect(place, (near[0], *across.values()), first, second, width)
    return (attended, *grads, grad_x)


def solution(mesh):
    fine = Mesh(mesh.devices.reshape(N, N, N, 2), ("y", "z", "x", "c"))
    seq, head = ("y", "z"), ("x", "c")
    in_specs = (P(seq, None), P(None, head), P(None, head), P(None, head), P(head, None, None), P(seq, head))
    out_specs = (P(seq, head),) * 5

    return jax.shard_map(shards, mesh=fine, in_specs=in_specs, out_specs=out_specs, check_vma=False)
```

```python
import jax
import jax.numpy as jnp
from jax import lax
from jax.experimental import pallas as pl
from jax.experimental.pallas import tpu as pltpu
from jax.sharding import Mesh, PartitionSpec as P


HEAD_DIM = 128
N = 4
SPLIT = 7
F32 = jnp.float32
BF16 = jnp.bfloat16
NT = (((1,), (1,)), ((), ()))
TN = (((0,), (0,)), ((), ()))


def shift(value, axis, by):
    n = lax.axis_size(axis)
    return lax.ppermute(value, axis, [(i, (i + by) % n) for i in range(n)])


def dot(a, b, dims=(((1,), (0,)), ((), ()))):
    return lax.dot_general(a, b, dims, preferred_element_type=F32)


def shape(*dims, dtype=BF16):
    return jax.ShapeDtypeStruct(dims, dtype)


def in_hbm(array):
    return pltpu.with_memory_space_constraint(array, pltpu.HBM)


def whole_call(body, ins, outs, mib=16):
    vmem = pl.BlockSpec(memory_space=pltpu.VMEM)
    smem = pl.BlockSpec(memory_space=pltpu.SMEM)
    return pl.pallas_call(
        body,
        out_shape=outs,
        in_specs=[smem if i.dtype == jnp.int32 else vmem for i in ins],
        out_specs=[vmem] * len(outs),
        compiler_params=pltpu.CompilerParams(vmem_limit_bytes=mib << 20),
    )(*ins)


def project(inputs, wq, wk, wv):
    rows, _ = inputs.shape
    q = (dot(inputs, wq) * HEAD_DIM ** (-0.5)).astype(BF16)
    k = (dot(inputs, wk) * (rows * N * N) ** (-0.5)).astype(BF16)
    return q, k, dot(inputs, wv).astype(BF16)


def block_sums(q, k, v, g):
    heads = q.shape[1] // HEAD_DIM

    def body(q, k, v, g, both):
        for h in range(heads):
            at = slice(h * HEAD_DIM, (h + 1) * HEAD_DIM)
            both[0, h] = dot(k[:, at], v[:, at], TN).astype(BF16)
            both[1, h] = dot(q[:, at], g[:, at], TN).astype(BF16)

    return whole_call(body, (q, k, v, g), [shape(2, heads, HEAD_DIM, HEAD_DIM)])[0]


def turn(place, inputs):
    rows, model = inputs.shape
    blk = model // (N * N)
    half = blk // 2
    part = model // N

    def body(place, x_hbm, *refs):
        outs, (x, pieces, x_sem, out_sem) = refs[:10], refs[10:]

        def lanes(s2):
            return pl.ds(pl.multiple_of(lax.rem(place[0] + s2, N) * part, 128), part)

        def load(s2):
            return pltpu.make_async_copy(x_hbm.at[:, lanes(s2)], x.at[:, lanes(s2)], x_sem.at[s2])

        def store(p):
            source = pieces.at[p]
            if p == 2:
                source = pieces.at[p, pl.ds(pl.multiple_of(lax.rem(place[2], 2) * blk, 128), blk)]
            return pltpu.make_async_copy(source, outs[p], out_sem.at[p])

        for s2 in range(N):
            load(s2).start()
        low = place[3] == 0
        for s2 in range(N):
            load(s2).wait()
            for s1 in range(N):
                block = lax.rem(place[0] + s2, N) * N + lax.rem(place[1] + s1, N)
                turned = x[:, pl.ds(pl.multiple_of(block * blk, 128), blk)].T
                mine = jnp.where(low, turned[:half], turned[half:])
                theirs = jnp.where(low, turned[half:], turned[:half])
                at1 = slice(s2 * half, (s2 + 1) * half)
                at2 = slice(s1 * half, (s1 + 1) * half)
                pieces[s1, at1] = mine
                pieces[4 + s2, at2] = mine
                if s1 == 0:
                    pieces[8, at1] = theirs
                if s2 == 0:
                    pieces[9, at2] = theirs
            store(4 + s2).start()
        for p in (0, 1, 2, 3, 8, 9):
            store(p).start()
        for p in range(10):
            store(p).wait()

    hbm = pl.BlockSpec(memory_space=pltpu.HBM)
    piece = (N * half, rows)
    return pl.pallas_call(
        body,
        out_shape=[pltpu.HBM((blk, rows) if p == 2 else piece, BF16) for p in range(10)],
        in_specs=[pl.BlockSpec(memory_space=pltpu.SMEM), hbm],
        out_specs=[hbm] * 10,
        scratch_shapes=[
            pltpu.VMEM(inputs.shape, BF16),
            pltpu.VMEM((10, *piece), BF16),
            pltpu.SemaphoreType.DMA((N,)),
            pltpu.SemaphoreType.DMA((10,)),
        ],
        compiler_params=pltpu.CompilerParams(vmem_limit_bytes=16 << 20),
        name="turn",
    )(place, in_hbm(inputs))


def local_part(q, k, v, g):
    rows, width = q.shape

    def body(q, k, v, g, att, gq, gk, gv):
        keep = lax.broadcasted_iota(jnp.int32, (rows, rows), 0) >= lax.broadcasted_iota(
            jnp.int32, (rows, rows), 1
        )
        for h in range(0, width, HEAD_DIM):
            at = slice(h, h + HEAD_DIM)
            qh, kh, vh, gh = q[:, at], k[:, at], v[:, at], g[:, at]
            causal = jnp.where(keep, dot(qh, kh, NT), 0.0).astype(BF16)
            back = jnp.where(keep, dot(gh, vh, NT), 0.0).astype(BF16)
            att[:, at] = dot(causal, vh)
            gq[:, at] = dot(back, kh)
            gk[:, at] = dot(back, qh, TN)
            gv[:, at] = dot(causal, gh, TN)

    return whole_call(body, (q, k, v, g), [shape(rows, width, dtype=F32)] * 4)


def row_sums(place, both, got, state_in):
    heads = state_in.shape[0]

    def body(place, both, r1, r2, r3, state, *outs):
        total = both[...].astype(F32)
        prior = state[...]
        later = jnp.zeros_like(prior)
        for s, ref in ((1, r1), (2, r2), (3, r3)):
            new = ref[...].astype(F32)
            total = total + new
            lower = s <= place[1]
            prior = prior + jnp.where(lower, new[0], 0.0)
            later = later + jnp.where(lower, 0.0, new[1])
        for s in (1, 2, 3):
            outs[s - 1][...] = jnp.where(place[0] + s < N, total[0], total[1]).astype(BF16)
        outs[3][...] = prior
        outs[4][...] = later

    mat = (heads, HEAD_DIM, HEAD_DIM)
    return whole_call(body, (place, both, *got, state_in), [shape(*mat)] * 3 + [shape(*mat, dtype=F32)] * 2)


def finish(place, q, k, v, g, local, prior, later, came):
    rows, width = q.shape
    heads = width // HEAD_DIM
    q_scale = HEAD_DIM ** (-0.5)
    k_scale = (rows * N * N) ** (-0.5)

    def body(place, q, k, v, g, la, lq, lk, lv, before, after, c1, c2, c3, att, g1, g2):
        for h in range(heads):
            prior = before[h]
            later = after[h]
            for s, ref in ((1, c1), (2, c2), (3, c3)):
                new = ref[h].astype(F32)
                lower = s <= place[0]
                prior = prior + jnp.where(lower, new, 0.0)
                later = later + jnp.where(lower, 0.0, new)
            prior = prior.astype(BF16)
            later = later.astype(BF16)
            at = slice(h * HEAD_DIM, (h + 1) * HEAD_DIM)
            qh, kh, vh, gh = q[:, at], k[:, at], v[:, at], g[:, at]
            att[:, at] = (la[:, at] + dot(qh, prior)).astype(BF16)
            new = (
                (lq[:, at] + dot(gh, prior, NT)) * q_scale,
                (lk[:, at] + dot(vh, later, NT)) * k_scale,
                lv[:, at] + dot(kh, later),
            )
            for n in range(3):
                t = h * 3 + n
                ref, to = (g1, t) if t < SPLIT else (g2, t - SPLIT)
                ref[:, to * HEAD_DIM : (to + 1) * HEAD_DIM] = new[n].astype(BF16)

    return whole_call(
        body,
        (place, q, k, v, g, *local, prior, later, *came),
        [shape(rows, width), shape(rows, SPLIT * HEAD_DIM), shape(rows, 3 * width - SPLIT * HEAD_DIM)],
    )


def far_project(place, g1, g2, wq, wk, wv):
    rows = g1.shape[0]
    model, width = wq.shape
    blk = model // (2 * N)

    def body(place, g1, g2, a, b, c, out, mine, grads, w, kept, far_sem, near_sem):
        def fetch(i, n, core, to, sem):
            first = (lax.rem(place[2] + i, N) * 2 + core) * blk
            return pltpu.make_async_copy(
                (a, b, c)[n].at[pl.ds(pl.multiple_of(first, 16), blk)],
                to.at[i, :, n * width : (n + 1) * width],
                sem.at[i, n],
            )

        def far(i, n):
            return fetch(i, n, 1 - place[3], w, far_sem)

        def near(i, n):
            return fetch(i, n, place[3], kept, near_sem)

        for i in range(N):
            for n in range(3):
                far(i, n).start()
        for p, ref in enumerate((g1, g2)):
            for at in range(ref.shape[1] // HEAD_DIM):
                t = p * SPLIT + at
                to = (t % 3) * width + t // 3 * HEAD_DIM
                grads[to : to + HEAD_DIM] = ref[:, at * HEAD_DIM : (at + 1) * HEAD_DIM].T
        for i in range(N):
            for n in range(3):
                far(i, n).wait()
            for n in range(3):
                near(i, n).start()
            out[i] = dot(w[i], grads[...]).astype(BF16)
        for i in range(N):
            for n in range(3):
                near(i, n).wait()
            mine[i] = dot(kept[i], grads[...]).astype(BF16)

    hbm = pl.BlockSpec(memory_space=pltpu.HBM)
    vmem = pl.BlockSpec(memory_space=pltpu.VMEM)
    return pl.pallas_call(
        body,
        out_shape=[shape(N, blk, rows)] * 2,
        in_specs=[pl.BlockSpec(memory_space=pltpu.SMEM), vmem, vmem] + [hbm] * 3,
        out_specs=[vmem] * 2,
        scratch_shapes=[
            pltpu.VMEM((3 * width, rows), BF16),
            pltpu.VMEM((N, blk, 3 * width), BF16),
            pltpu.VMEM((N, blk, 3 * width), BF16),
            pltpu.SemaphoreType.DMA((N, 3)),
            pltpu.SemaphoreType.DMA((N, 3)),
        ],
        compiler_params=pltpu.CompilerParams(vmem_limit_bytes=28 << 20),
        name="far",
    )(place, g1, g2, *map(in_hbm, (wq, wk, wv)))


def near_sum(mine, received):
    _, blk, rows = mine.shape

    def body(mine, received, *outs):
        for s in range(N):
            outs[s][...] = (mine[s].astype(F32) + received[s].astype(F32)).astype(BF16)

    return whole_call(body, (mine, received), [shape(blk, rows)] * N)


def weight_blocks(place, mine, theirs, rhs):
    groups = [[p if isinstance(p, tuple) else (p,) for p in group] for group in (mine, theirs)]
    half = mine[0].shape[0] // N
    cols = rhs[0].shape[1]

    def body(place, *refs):
        refs = list(refs)
        even = lax.rem(place[2], 2) == 0

        def take(pieces):
            values = [refs.pop(0)[...] for _ in pieces]
            if len(values) == 1:
                return values[0]
            a, b = values
            return jnp.concatenate([jnp.where(even, a, b), jnp.where(even, b, a)], 0)

        lefts = [jnp.concatenate([take(pieces) for pieces in group], 1) for group in groups]
        right = jnp.concatenate([refs.pop(0)[...] for _ in range(N)], 0)
        for n in range(2):
            total = dot(lefts[n], right).astype(BF16)
            for s in range(N):
                refs[s][n * half : (n + 1) * half] = total[s * half : (s + 1) * half]

    flat = [a for group in groups for pieces in group for a in pieces]
    return whole_call(body, (place, *flat, *rhs), [shape(2 * half, cols)] * N)


def collect(place, across, first, second, width):
    rows = across[0].shape[1]
    model = across[0].shape[0]
    blk = first[0].shape[0]
    half = blk // 2

    def body(place, *refs):
        grad_x, *outs = refs[3 * N :]

        def total(which, rows=slice(None)):
            value = refs[which * N][rows].astype(F32)
            for ref in refs[which * N + 1 : which * N + N]:
                value = value + ref[rows].astype(F32)
            return value.astype(BF16)

        grad_x[...] = total(0).T
        for n in range(2):
            core = place[3] if n == 0 else 1 - place[3]
            to = pl.ds(pl.multiple_of(core * half, 64), half)
            for which, start in ((1, 0), (2, SPLIT)):
                value = total(which, slice(n * half, (n + 1) * half))
                for at in range(value.shape[1] // HEAD_DIM):
                    h, m = divmod(start + at, 3)
                    outs[m][to, h * HEAD_DIM : (h + 1) * HEAD_DIM] = value[:, at * HEAD_DIM : (at + 1) * HEAD_DIM]

    return whole_call(body, (place, *across, *first, *second), [shape(rows, model)] + [shape(blk, width)] * 3)


def shards(inputs, w_query, w_key, w_value, state_in, grad_out):
    width = w_query.shape[1]
    order = (1, 3, 2)
    three = (1, 2, 3)

    place = jnp.stack([lax.axis_index(a) for a in ("y", "z", "x", "c")]).astype(jnp.int32)
    pieces = turn(place, inputs)
    q, k, v = project(inputs, w_query, w_key, w_value)
    both = block_sums(q, k, v, grad_out)
    got = {s: shift(both, "z", s) for s in order}

    local = local_part(q, k, v, grad_out)
    *out, prior, later = row_sums(place, both, [got[s] for s in three], state_in)
    came = {s: shift(out[s - 1], "y", s) for s in order}

    mine1 = {s: shift(pieces[s], "z", s) for s in order}
    mine2 = {s: shift(pieces[4 + s], "y", s) for s in order}
    other = lax.ppermute(mine1[2], "x", [(i, i ^ 1) for i in range(N)])
    theirs1 = {s: shift(mine1[s], "c", 1) for s in order}
    mine1[2], theirs1[2] = (mine1[2], other), (theirs1[2], shift(other, "c", 1))
    theirs2 = {s: shift(mine2[s], "c", 1) for s in order}
    mine1[0], mine2[0], theirs1[0], theirs2[0] = pieces[0], pieces[4], pieces[8], pieces[9]

    attended, g1, g2 = finish(
        place, q, k, v, grad_out, local, prior, later, [came[s] for s in three]
    )
    rhs1 = {s: shift(g1, "z", s) for s in order}
    rhs2 = {s: shift(g2, "y", s) for s in order}
    rhs1[0], rhs2[0] = g1, g2

    far, mine = far_project(place, g1, g2, w_query, w_key, w_value)
    far = shift(far, "c", 1)
    near = near_sum(mine, far)
    across = {s: shift(near[s], "x", s) for s in order}

    def scattered(mine, theirs, rhs, axis):
        blocks = weight_blocks(place, *([a[s] for s in range(N)] for a in (mine, theirs, rhs)))
        return [blocks[0]] + [shift(blocks[s], axis, s) for s in order]

    first = scattered(mine1, theirs1, rhs1, "y")
    second = scattered(mine2, theirs2, rhs2, "z")
    grad_x, *grads = collect(place, (near[0], *across.values()), first, second, width)
    return (attended, *grads, grad_x)


def solution(mesh):
    fine = Mesh(mesh.devices.reshape(N, N, N, 2), ("y", "z", "x", "c"))
    seq, head = ("y", "z"), ("x", "c")
    in_specs = (P(seq, None), P(None, head), P(None, head), P(None, head), P(head, None, None), P(seq, head))
    out_specs = (P(seq, head),) * 5

    return jax.shard_map(shards, mesh=fine, in_specs=in_specs, out_specs=out_specs, check_vma=False)
```

```python
import jax
import jax.numpy as jnp
from jax import lax
from jax.experimental import pallas as pl
from jax.experimental.pallas import tpu as pltpu
from jax.sharding import Mesh, PartitionSpec as P


HEAD_DIM = 128
N = 4
SPLIT = 7
F32 = jnp.float32
BF16 = jnp.bfloat16
NT = (((1,), (1,)), ((), ()))
TN = (((0,), (0,)), ((), ()))


def shift(value, axis, by):
    n = lax.axis_size(axis)
    return lax.ppermute(value, axis, [(i, (i + by) % n) for i in range(n)])


def dot(a, b, dims=(((1,), (0,)), ((), ()))):
    return lax.dot_general(a, b, dims, preferred_element_type=F32)


def shape(*dims, dtype=BF16):
    return jax.ShapeDtypeStruct(dims, dtype)


def in_hbm(array):
    return pltpu.with_memory_space_constraint(array, pltpu.HBM)


def whole_call(body, ins, outs, mib=16):
    vmem = pl.BlockSpec(memory_space=pltpu.VMEM)
    smem = pl.BlockSpec(memory_space=pltpu.SMEM)
    return pl.pallas_call(
        body,
        out_shape=outs,
        in_specs=[smem if i.dtype == jnp.int32 else vmem for i in ins],
        out_specs=[vmem] * len(outs),
        compiler_params=pltpu.CompilerParams(vmem_limit_bytes=mib << 20),
    )(*ins)


def project(inputs, wq, wk, wv):
    rows, _ = inputs.shape
    q = (dot(inputs, wq) * HEAD_DIM ** (-0.5)).astype(BF16)
    k = (dot(inputs, wk) * (rows * N * N) ** (-0.5)).astype(BF16)
    return q, k, dot(inputs, wv).astype(BF16)


def block_sums(q, k, v, g):
    heads = q.shape[1] // HEAD_DIM

    def body(q, k, v, g, both):
        for h in range(heads):
            at = slice(h * HEAD_DIM, (h + 1) * HEAD_DIM)
            both[0, h] = dot(k[:, at], v[:, at], TN).astype(BF16)
            both[1, h] = dot(q[:, at], g[:, at], TN).astype(BF16)

    return whole_call(body, (q, k, v, g), [shape(2, heads, HEAD_DIM, HEAD_DIM)])[0]


def turn(place, inputs):
    rows, model = inputs.shape
    blk = model // (N * N)
    half = blk // 2
    part = model // N

    def body(place, x_hbm, *refs):
        outs, (x, pieces, x_sem, out_sem) = refs[:10], refs[10:]

        def lanes(s2):
            return pl.ds(pl.multiple_of(lax.rem(place[0] + s2, N) * part, 128), part)

        def load(s2):
            return pltpu.make_async_copy(x_hbm.at[:, lanes(s2)], x.at[:, lanes(s2)], x_sem.at[s2])

        def store(p):
            source = pieces.at[p]
            if p == 2:
                source = pieces.at[p, pl.ds(pl.multiple_of(lax.rem(place[2], 2) * blk, 128), blk)]
            return pltpu.make_async_copy(source, outs[p], out_sem.at[p])

        for s2 in range(N):
            load(s2).start()
        low = place[3] == 0
        for s2 in range(N):
            load(s2).wait()
            for s1 in range(N):
                block = lax.rem(place[0] + s2, N) * N + lax.rem(place[1] + s1, N)
                turned = x[:, pl.ds(pl.multiple_of(block * blk, 128), blk)].T
                mine = jnp.where(low, turned[:half], turned[half:])
                theirs = jnp.where(low, turned[half:], turned[:half])
                at1 = slice(s2 * half, (s2 + 1) * half)
                at2 = slice(s1 * half, (s1 + 1) * half)
                pieces[s1, at1] = mine
                pieces[4 + s2, at2] = mine
                if s1 == 0:
                    pieces[8, at1] = theirs
                if s2 == 0:
                    pieces[9, at2] = theirs
            store(4 + s2).start()
        for p in (0, 1, 2, 3, 8, 9):
            store(p).start()
        for p in range(10):
            store(p).wait()

    hbm = pl.BlockSpec(memory_space=pltpu.HBM)
    piece = (N * half, rows)
    return pl.pallas_call(
        body,
        out_shape=[pltpu.HBM((blk, rows) if p == 2 else piece, BF16) for p in range(10)],
        in_specs=[pl.BlockSpec(memory_space=pltpu.SMEM), hbm],
        out_specs=[hbm] * 10,
        scratch_shapes=[
            pltpu.VMEM(inputs.shape, BF16),
            pltpu.VMEM((10, *piece), BF16),
            pltpu.SemaphoreType.DMA((N,)),
            pltpu.SemaphoreType.DMA((10,)),
        ],
        compiler_params=pltpu.CompilerParams(vmem_limit_bytes=16 << 20),
        name="turn",
    )(place, in_hbm(inputs))


def local_part(q, k, v, g):
    rows, width = q.shape

    def body(q, k, v, g, att, gq, gk, gv):
        keep = lax.broadcasted_iota(jnp.int32, (rows, rows), 0) >= lax.broadcasted_iota(
            jnp.int32, (rows, rows), 1
        )
        for h in range(0, width, HEAD_DIM):
            at = slice(h, h + HEAD_DIM)
            qh, kh, vh, gh = q[:, at], k[:, at], v[:, at], g[:, at]
            causal = jnp.where(keep, dot(qh, kh, NT), 0.0).astype(BF16)
            back = jnp.where(keep, dot(gh, vh, NT), 0.0).astype(BF16)
            att[:, at] = dot(causal, vh)
            gq[:, at] = dot(back, kh)
            gk[:, at] = dot(back, qh, TN)
            gv[:, at] = dot(causal, gh, TN)

    return whole_call(body, (q, k, v, g), [shape(rows, width, dtype=F32)] * 4)


def row_sums(place, both, got, state_in):
    heads = state_in.shape[0]

    def body(place, both, r1, r2, r3, state, *outs):
        total = both[...].astype(F32)
        prior = state[...]
        later = jnp.zeros_like(prior)
        for s, ref in ((1, r1), (2, r2), (3, r3)):
            new = ref[...].astype(F32)
            total = total + new
            lower = s <= place[1]
            prior = prior + jnp.where(lower, new[0], 0.0)
            later = later + jnp.where(lower, 0.0, new[1])
        for s in (1, 2, 3):
            outs[s - 1][...] = jnp.where(place[0] + s < N, total[0], total[1]).astype(BF16)
        outs[3][...] = prior
        outs[4][...] = later

    mat = (heads, HEAD_DIM, HEAD_DIM)
    return whole_call(body, (place, both, *got, state_in), [shape(*mat)] * 3 + [shape(*mat, dtype=F32)] * 2)


def finish(place, q, k, v, g, local, prior, later, came):
    rows, width = q.shape
    heads = width // HEAD_DIM
    q_scale = HEAD_DIM ** (-0.5)
    k_scale = (rows * N * N) ** (-0.5)

    def body(place, q, k, v, g, la, lq, lk, lv, before, after, c1, c2, c3, att, g1, g2):
        for h in range(heads):
            prior = before[h]
            later = after[h]
            for s, ref in ((1, c1), (2, c2), (3, c3)):
                new = ref[h].astype(F32)
                lower = s <= place[0]
                prior = prior + jnp.where(lower, new, 0.0)
                later = later + jnp.where(lower, 0.0, new)
            prior = prior.astype(BF16)
            later = later.astype(BF16)
            at = slice(h * HEAD_DIM, (h + 1) * HEAD_DIM)
            qh, kh, vh, gh = q[:, at], k[:, at], v[:, at], g[:, at]
            att[:, at] = (la[:, at] + dot(qh, prior)).astype(BF16)
            new = (
                (lq[:, at] + dot(gh, prior, NT)) * q_scale,
                (lk[:, at] + dot(vh, later, NT)) * k_scale,
                lv[:, at] + dot(kh, later),
            )
            for n in range(3):
                t = h * 3 + n
                ref, to = (g1, t) if t < SPLIT else (g2, t - SPLIT)
                ref[:, to * HEAD_DIM : (to + 1) * HEAD_DIM] = new[n].astype(BF16)

    return whole_call(
        body,
        (place, q, k, v, g, *local, prior, later, *came),
        [shape(rows, width), shape(rows, SPLIT * HEAD_DIM), shape(rows, 3 * width - SPLIT * HEAD_DIM)],
    )


def far_project(place, g1, g2, wq, wk, wv):
    rows = g1.shape[0]
    model, width = wq.shape
    blk = model // (2 * N)

    def body(place, g1, g2, a, b, c, out, kept, grads, w, far_sem, near_sem):
        def fetch(i, n, core, to, sem):
            first = (lax.rem(place[2] + i, N) * 2 + core) * blk
            return pltpu.make_async_copy(
                (a, b, c)[n].at[pl.ds(pl.multiple_of(first, 16), blk)],
                to.at[i, :, n * width : (n + 1) * width],
                sem.at[i, n],
            )

        def far(i, n):
            return fetch(i, n, 1 - place[3], w, far_sem)

        def near(i, n):
            return fetch(i, n, place[3], kept, near_sem)

        for i in range(N):
            for n in range(3):
                far(i, n).start()
        for p, ref in enumerate((g1, g2)):
            for at in range(ref.shape[1] // HEAD_DIM):
                t = p * SPLIT + at
                to = (t % 3) * width + t // 3 * HEAD_DIM
                grads[to : to + HEAD_DIM] = ref[:, at * HEAD_DIM : (at + 1) * HEAD_DIM].T
        for i in range(N):
            for n in range(3):
                far(i, n).wait()
            for n in range(3):
                near(i, n).start()
            out[i] = dot(w[i], grads[...]).astype(BF16)
        for i in range(N):
            for n in range(3):
                near(i, n).wait()

    hbm = pl.BlockSpec(memory_space=pltpu.HBM)
    vmem = pl.BlockSpec(memory_space=pltpu.VMEM)
    return pl.pallas_call(
        body,
        out_shape=[shape(N, blk, rows), pltpu.VMEM((N, blk, 3 * width), BF16), shape(3 * width, rows)],
        in_specs=[pl.BlockSpec(memory_space=pltpu.SMEM), vmem, vmem] + [hbm] * 3,
        out_specs=[vmem] * 3,
        scratch_shapes=[
            pltpu.VMEM((N, blk, 3 * width), BF16),
            pltpu.SemaphoreType.DMA((N, 3)),
            pltpu.SemaphoreType.DMA((N, 3)),
        ],
        compiler_params=pltpu.CompilerParams(vmem_limit_bytes=24 << 20),
        name="far",
    )(place, g1, g2, *map(in_hbm, (wq, wk, wv)))


def near_project(kept, grads, received):
    blk = kept.shape[1]
    rows = grads.shape[1]

    def body(kept, grads, received, *outs):
        for s in range(N):
            mine = dot(kept[s], grads[...]).astype(BF16).astype(F32)
            outs[s][...] = (mine + received[s].astype(F32)).astype(BF16)

    return whole_call(body, (kept, grads, received), [shape(blk, rows)] * N)


def weight_blocks(place, mine, theirs, rhs):
    groups = [[p if isinstance(p, tuple) else (p,) for p in group] for group in (mine, theirs)]
    half = mine[0].shape[0] // N
    cols = rhs[0].shape[1]

    def body(place, *refs):
        refs = list(refs)
        held = [[[refs.pop(0) for _ in pieces] for pieces in group] for group in groups]
        right = jnp.concatenate([refs.pop(0)[...] for _ in range(N)], 0)
        even = lax.rem(place[2], 2) == 0

        def take(pieces):
            if len(pieces) == 1:
                return pieces[0][...]
            a, b = pieces[0][...], pieces[1][...]
            return jnp.concatenate([jnp.where(even, a, b), jnp.where(even, b, a)], 0)

        for n in range(2):
            total = dot(jnp.concatenate([take(p) for p in held[n]], 1), right).astype(BF16)
            for s in range(N):
                refs[s][n * half : (n + 1) * half] = total[s * half : (s + 1) * half]

    flat = [a for group in groups for pieces in group for a in pieces]
    return whole_call(body, (place, *flat, *rhs), [shape(2 * half, cols)] * N)


def collect(place, across, first, second, width):
    rows = across[0].shape[1]
    model = across[0].shape[0]
    blk = first[0].shape[0]
    half = blk // 2

    def body(place, *refs):
        grad_x, *outs = refs[3 * N :]

        def total(which, rows=slice(None)):
            value = refs[which * N][rows].astype(F32)
            for ref in refs[which * N + 1 : which * N + N]:
                value = value + ref[rows].astype(F32)
            return value.astype(BF16)

        grad_x[...] = total(0).T
        for n in range(2):
            core = place[3] if n == 0 else 1 - place[3]
            to = pl.ds(pl.multiple_of(core * half, 64), half)
            for which, start in ((1, 0), (2, SPLIT)):
                value = total(which, slice(n * half, (n + 1) * half))
                for at in range(value.shape[1] // HEAD_DIM):
                    h, m = divmod(start + at, 3)
                    outs[m][to, h * HEAD_DIM : (h + 1) * HEAD_DIM] = value[:, at * HEAD_DIM : (at + 1) * HEAD_DIM]

    return whole_call(body, (place, *across, *first, *second), [shape(rows, model)] + [shape(blk, width)] * 3)


def shards(inputs, w_query, w_key, w_value, state_in, grad_out):
    width = w_query.shape[1]
    order = (1, 3, 2)
    three = (1, 2, 3)

    place = jnp.stack([lax.axis_index(a) for a in ("y", "z", "x", "c")]).astype(jnp.int32)
    pieces = turn(place, inputs)
    q, k, v = project(inputs, w_query, w_key, w_value)
    both = block_sums(q, k, v, grad_out)
    got = {s: shift(both, "z", s) for s in order}

    local = local_part(q, k, v, grad_out)
    *out, prior, later = row_sums(place, both, [got[s] for s in three], state_in)
    came = {s: shift(out[s - 1], "y", s) for s in order}

    mine1 = {s: shift(pieces[s], "z", s) for s in order}
    mine2 = {s: shift(pieces[4 + s], "y", s) for s in order}
    other = lax.ppermute(mine1[2], "x", [(i, i ^ 1) for i in range(N)])
    theirs1 = {s: shift(mine1[s], "c", 1) for s in order}
    mine1[2], theirs1[2] = (mine1[2], other), (theirs1[2], shift(other, "c", 1))
    theirs2 = {s: shift(mine2[s], "c", 1) for s in order}
    mine1[0], mine2[0], theirs1[0], theirs2[0] = pieces[0], pieces[4], pieces[8], pieces[9]

    attended, g1, g2 = finish(
        place, q, k, v, grad_out, local, prior, later, [came[s] for s in three]
    )
    rhs1 = {s: shift(g1, "z", s) for s in order}
    rhs2 = {s: shift(g2, "y", s) for s in order}
    rhs1[0], rhs2[0] = g1, g2

    far, kept, turned = far_project(place, g1, g2, w_query, w_key, w_value)
    far = shift(far, "c", 1)
    near = near_project(kept, turned, far)
    across = {s: shift(near[s], "x", s) for s in order}

    def scattered(mine, theirs, rhs, axis):
        blocks = weight_blocks(place, *([a[s] for s in range(N)] for a in (mine, theirs, rhs)))
        return [blocks[0]] + [shift(blocks[s], axis, s) for s in order]

    first = scattered(mine1, theirs1, rhs1, "y")
    second = scattered(mine2, theirs2, rhs2, "z")
    grad_x, *grads = collect(place, (near[0], *across.values()), first, second, width)
    return (attended, *grads, grad_x)


def solution(mesh):
    fine = Mesh(mesh.devices.reshape(N, N, N, 2), ("y", "z", "x", "c"))
    seq, head = ("y", "z"), ("x", "c")
    in_specs = (P(seq, None), P(None, head), P(None, head), P(None, head), P(head, None, None), P(seq, head))
    out_specs = (P(seq, head),) * 5

    return jax.shard_map(shards, mesh=fine, in_specs=in_specs, out_specs=out_specs, check_vma=False)
```

```python
import jax
import jax.numpy as jnp
from jax import lax
from jax.experimental import pallas as pl
from jax.experimental.pallas import tpu as pltpu
from jax.sharding import Mesh, PartitionSpec as P


HEAD_DIM = 128
N = 4
SPLIT = 7
F32 = jnp.float32
BF16 = jnp.bfloat16
NT = (((1,), (1,)), ((), ()))
TN = (((0,), (0,)), ((), ()))


def shift(value, axis, by):
    n = lax.axis_size(axis)
    return lax.ppermute(value, axis, [(i, (i + by) % n) for i in range(n)])


def dot(a, b, dims=(((1,), (0,)), ((), ()))):
    return lax.dot_general(a, b, dims, preferred_element_type=F32)


def shape(*dims, dtype=BF16):
    return jax.ShapeDtypeStruct(dims, dtype)


def here():
    return [lax.axis_index(axis) for axis in ("y", "z", "x", "c")]


def in_hbm(array):
    return pltpu.with_memory_space_constraint(array, pltpu.HBM)


def whole_call(body, ins, outs, mib=16):
    vmem = pl.BlockSpec(memory_space=pltpu.VMEM)
    smem = pl.BlockSpec(memory_space=pltpu.SMEM)
    return pl.pallas_call(
        body,
        out_shape=outs,
        in_specs=[smem if i.dtype == jnp.int32 else vmem for i in ins],
        out_specs=[vmem] * len(outs),
        compiler_params=pltpu.CompilerParams(vmem_limit_bytes=mib << 20),
    )(*ins)


def project(inputs, wq, wk, wv):
    rows, _ = inputs.shape
    q = (dot(inputs, wq) * HEAD_DIM ** (-0.5)).astype(BF16)
    k = (dot(inputs, wk) * (rows * N * N) ** (-0.5)).astype(BF16)
    return q, k, dot(inputs, wv).astype(BF16)


def block_sums(q, k, v, g):
    heads = q.shape[1] // HEAD_DIM

    def body(q, k, v, g, both):
        for h in range(heads):
            at = slice(h * HEAD_DIM, (h + 1) * HEAD_DIM)
            both[0, h] = dot(k[:, at], v[:, at], TN).astype(BF16)
            both[1, h] = dot(q[:, at], g[:, at], TN).astype(BF16)

    return whole_call(body, (q, k, v, g), [shape(2, heads, HEAD_DIM, HEAD_DIM)])[0]


def turn(inputs):
    rows, model = inputs.shape
    blk = model // (N * N)
    half = blk // 2
    part = model // N

    def body(x_hbm, *refs):
        place = here()
        outs, (x, pieces, x_sem, out_sem) = refs[:10], refs[10:]

        def lanes(s2):
            return pl.ds(pl.multiple_of(lax.rem(place[0] + s2, N) * part, 128), part)

        def load(s2):
            return pltpu.make_async_copy(x_hbm.at[:, lanes(s2)], x.at[:, lanes(s2)], x_sem.at[s2])

        def store(p):
            return pltpu.make_async_copy(pieces.at[p], outs[p], out_sem.at[p])

        for s2 in range(N):
            load(s2).start()
        low = place[3] == 0
        for s2 in range(N):
            load(s2).wait()
            for s1 in range(N):
                block = lax.rem(place[0] + s2, N) * N + lax.rem(place[1] + s1, N)
                turned = x[:, pl.ds(pl.multiple_of(block * blk, 128), blk)].T
                mine = jnp.where(low, turned[:half], turned[half:])
                theirs = jnp.where(low, turned[half:], turned[:half])
                at1 = slice(s2 * half, (s2 + 1) * half)
                at2 = slice(s1 * half, (s1 + 1) * half)
                pieces[s1, at1] = mine
                pieces[4 + s2, at2] = mine
                if s1 == 0:
                    pieces[8, at1] = theirs
                if s2 == 0:
                    pieces[9, at2] = theirs
            store(4 + s2).start()
        for p in (0, 1, 2, 3, 8, 9):
            store(p).start()
        for p in range(10):
            store(p).wait()

    hbm = pl.BlockSpec(memory_space=pltpu.HBM)
    piece = (N * half, rows)
    return pl.pallas_call(
        body,
        out_shape=[pltpu.HBM(piece, BF16)] * 10,
        in_specs=[hbm],
        out_specs=[hbm] * 10,
        scratch_shapes=[
            pltpu.VMEM(inputs.shape, BF16),
            pltpu.VMEM((10, *piece), BF16),
            pltpu.SemaphoreType.DMA((N,)),
            pltpu.SemaphoreType.DMA((10,)),
        ],
        compiler_params=pltpu.CompilerParams(vmem_limit_bytes=16 << 20),
        name="turn",
    )(in_hbm(inputs))


def local_part(q, k, v, g):
    rows, width = q.shape

    def body(q, k, v, g, att, gq, gk, gv):
        keep = lax.broadcasted_iota(jnp.int32, (rows, rows), 0) >= lax.broadcasted_iota(
            jnp.int32, (rows, rows), 1
        )
        for h in range(0, width, HEAD_DIM):
            at = slice(h, h + HEAD_DIM)
            qh, kh, vh, gh = q[:, at], k[:, at], v[:, at], g[:, at]
            causal = jnp.where(keep, dot(qh, kh, NT), 0.0).astype(BF16)
            back = jnp.where(keep, dot(gh, vh, NT), 0.0).astype(BF16)
            att[:, at] = dot(causal, vh)
            gq[:, at] = dot(back, kh)
            gk[:, at] = dot(back, qh, TN)
            gv[:, at] = dot(causal, gh, TN)

    return whole_call(body, (q, k, v, g), [shape(rows, width, dtype=F32)] * 4)


def row_sums(both, got, state_in):
    heads = state_in.shape[0]

    def body(both, r1, r2, r3, state, *outs):
        place = here()
        total = both[...].astype(F32)
        prior = state[...]
        later = jnp.zeros_like(prior)
        for s, ref in ((1, r1), (2, r2), (3, r3)):
            new = ref[...].astype(F32)
            total = total + new
            lower = s <= place[1]
            prior = prior + jnp.where(lower, new[0], 0.0)
            later = later + jnp.where(lower, 0.0, new[1])
        for s in (1, 2, 3):
            outs[s - 1][...] = jnp.where(place[0] + s < N, total[0], total[1]).astype(BF16)
        outs[3][...] = prior
        outs[4][...] = later

    mat = (heads, HEAD_DIM, HEAD_DIM)
    return whole_call(body, (both, *got, state_in), [shape(*mat)] * 3 + [shape(*mat, dtype=F32)] * 2)


def finish(q, k, v, g, local, prior, later, came):
    rows, width = q.shape
    heads = width // HEAD_DIM
    q_scale = HEAD_DIM ** (-0.5)
    k_scale = (rows * N * N) ** (-0.5)

    def body(q, k, v, g, la, lq, lk, lv, before, after, c1, c2, c3, att, g1, g2):
        place = here()
        for h in range(heads):
            prior = before[h]
            later = after[h]
            for s, ref in ((1, c1), (2, c2), (3, c3)):
                new = ref[h].astype(F32)
                lower = s <= place[0]
                prior = prior + jnp.where(lower, new, 0.0)
                later = later + jnp.where(lower, 0.0, new)
            prior = prior.astype(BF16)
            later = later.astype(BF16)
            at = slice(h * HEAD_DIM, (h + 1) * HEAD_DIM)
            qh, kh, vh, gh = q[:, at], k[:, at], v[:, at], g[:, at]
            att[:, at] = (la[:, at] + dot(qh, prior)).astype(BF16)
            new = (
                (lq[:, at] + dot(gh, prior, NT)) * q_scale,
                (lk[:, at] + dot(vh, later, NT)) * k_scale,
                lv[:, at] + dot(kh, later),
            )
            for n in range(3):
                t = h * 3 + n
                ref, to = (g1, t) if t < SPLIT else (g2, t - SPLIT)
                ref[:, to * HEAD_DIM : (to + 1) * HEAD_DIM] = new[n].astype(BF16)

    return whole_call(
        body,
        (q, k, v, g, *local, prior, later, *came),
        [shape(rows, width), shape(rows, SPLIT * HEAD_DIM), shape(rows, 3 * width - SPLIT * HEAD_DIM)],
    )


def far_project(g1, g2, wq, wk, wv):
    rows = g1.shape[0]
    model, width = wq.shape
    blk = model // (2 * N)

    def body(g1, g2, a, b, c, out, kept, grads, w, far_sem, near_sem):
        place = here()

        def fetch(i, n, core, to, sem):
            first = (lax.rem(place[2] + i, N) * 2 + core) * blk
            return pltpu.make_async_copy(
                (a, b, c)[n].at[pl.ds(pl.multiple_of(first, 16), blk)],
                to.at[i, :, n * width : (n + 1) * width],
                sem.at[i, n],
            )

        def far(i, n):
            return fetch(i, n, 1 - place[3], w, far_sem)

        def near(i, n):
            return fetch(i, n, place[3], kept, near_sem)

        for i in range(N):
            for n in range(3):
                far(i, n).start()
        for p, ref in enumerate((g1, g2)):
            for at in range(ref.shape[1] // HEAD_DIM):
                t = p * SPLIT + at
                to = (t % 3) * width + t // 3 * HEAD_DIM
                grads[to : to + HEAD_DIM] = ref[:, at * HEAD_DIM : (at + 1) * HEAD_DIM].T
        for i in range(N):
            for n in range(3):
                far(i, n).wait()
            for n in range(3):
                near(i, n).start()
            out[i] = dot(w[i], grads[...]).astype(BF16)
        for i in range(N):
            for n in range(3):
                near(i, n).wait()

    hbm = pl.BlockSpec(memory_space=pltpu.HBM)
    vmem = pl.BlockSpec(memory_space=pltpu.VMEM)
    return pl.pallas_call(
        body,
        out_shape=[shape(N, blk, rows), pltpu.VMEM((N, blk, 3 * width), BF16), shape(3 * width, rows)],
        in_specs=[vmem, vmem] + [hbm] * 3,
        out_specs=[vmem] * 3,
        scratch_shapes=[
            pltpu.VMEM((N, blk, 3 * width), BF16),
            pltpu.SemaphoreType.DMA((N, 3)),
            pltpu.SemaphoreType.DMA((N, 3)),
        ],
        compiler_params=pltpu.CompilerParams(vmem_limit_bytes=24 << 20),
        name="far",
    )(g1, g2, *map(in_hbm, (wq, wk, wv)))


def near_project(kept, grads, received):
    blk = kept.shape[1]
    rows = grads.shape[1]

    def body(kept, grads, received, *outs):
        for s in range(N):
            mine = dot(kept[s], grads[...]).astype(BF16).astype(F32)
            outs[s][...] = (mine + received[s].astype(F32)).astype(BF16)

    return whole_call(body, (kept, grads, received), [shape(blk, rows)] * N)


def weight_blocks(mine, theirs, rhs):
    half = mine[0].shape[0] // N
    cols = rhs[0].shape[1]

    def body(*refs):
        outs = refs[3 * N :]
        right = jnp.concatenate([r[...] for r in refs[2 * N : 3 * N]], 0)
        for n in range(2):
            left = jnp.concatenate([r[...] for r in refs[n * N : (n + 1) * N]], 1)
            total = dot(left, right).astype(BF16)
            for s in range(N):
                outs[s][n * half : (n + 1) * half] = total[s * half : (s + 1) * half]

    return whole_call(body, (*mine, *theirs, *rhs), [shape(2 * half, cols)] * N)


def collect(across, first, second, width):
    rows = across[0].shape[1]
    model = across[0].shape[0]
    blk = first[0].shape[0]
    half = blk // 2

    def body(*refs):
        place = here()
        grad_x, *outs = refs[3 * N :]

        def total(which, rows=slice(None)):
            value = refs[which * N][rows].astype(F32)
            for ref in refs[which * N + 1 : which * N + N]:
                value = value + ref[rows].astype(F32)
            return value.astype(BF16)

        grad_x[...] = total(0).T
        for n in range(2):
            core = place[3] if n == 0 else 1 - place[3]
            to = pl.ds(pl.multiple_of(core * half, 64), half)
            for which, start in ((1, 0), (2, SPLIT)):
                value = total(which, slice(n * half, (n + 1) * half))
                for at in range(value.shape[1] // HEAD_DIM):
                    h, m = divmod(start + at, 3)
                    outs[m][to, h * HEAD_DIM : (h + 1) * HEAD_DIM] = value[:, at * HEAD_DIM : (at + 1) * HEAD_DIM]

    return whole_call(body, (*across, *first, *second), [shape(rows, model)] + [shape(blk, width)] * 3)


def shards(inputs, w_query, w_key, w_value, state_in, grad_out):
    width = w_query.shape[1]
    order = (1, 3, 2)
    three = (1, 2, 3)

    pieces = turn(inputs)
    q, k, v = project(inputs, w_query, w_key, w_value)
    both = block_sums(q, k, v, grad_out)
    got = {s: shift(both, "z", s) for s in order}

    local = local_part(q, k, v, grad_out)
    *out, prior, later = row_sums(both, [got[s] for s in three], state_in)
    came = {s: shift(out[s - 1], "y", s) for s in order}

    mine1 = {s: shift(pieces[s], "z", s) for s in order}
    mine2 = {s: shift(pieces[4 + s], "y", s) for s in order}
    theirs1 = {s: shift(mine1[s], "c", 1) for s in order}
    theirs2 = {s: shift(mine2[s], "c", 1) for s in order}
    mine1[0], mine2[0], theirs1[0], theirs2[0] = pieces[0], pieces[4], pieces[8], pieces[9]

    attended, g1, g2 = finish(
        q, k, v, grad_out, local, prior, later, [came[s] for s in three]
    )
    rhs1 = {s: shift(g1, "z", s) for s in order}
    rhs2 = {s: shift(g2, "y", s) for s in order}
    rhs1[0], rhs2[0] = g1, g2

    far, kept, turned = far_project(g1, g2, w_query, w_key, w_value)
    far = shift(far, "c", 1)
    near = near_project(kept, turned, far)
    across = {s: shift(near[s], "x", s) for s in order}

    def scattered(mine, theirs, rhs, axis):
        blocks = weight_blocks(*([a[s] for s in range(N)] for a in (mine, theirs, rhs)))
        return [blocks[0]] + [shift(blocks[s], axis, s) for s in order]

    first = scattered(mine1, theirs1, rhs1, "y")
    second = scattered(mine2, theirs2, rhs2, "z")
    grad_x, *grads = collect((near[0], *across.values()), first, second, width)
    return (attended, *grads, grad_x)


def solution(mesh):
    fine = Mesh(mesh.devices.reshape(N, N, N, 2), ("y", "z", "x", "c"))
    seq, head = ("y", "z"), ("x", "c")
    in_specs = (P(seq, None), P(None, head), P(None, head), P(None, head), P(head, None, None), P(seq, head))
    out_specs = (P(seq, head),) * 5

    return jax.shard_map(shards, mesh=fine, in_specs=in_specs, out_specs=out_specs, check_vma=False)
```
